512 devices in a mesh: leaf: 64 (over x, y, core), grp: 8 (over z).
Axes of the slice: x: 4, y: 8, z: 8, core: 2. Of those that a mesh axis runs over, the one named last changes fastest.
Arguments:
- points: bfloat16 [256, 524288], P(None, ('leaf', 'grp')), may hold values from -6 to 6
- charges: bfloat16 [64, 524288], P(None, ('leaf', 'grp')), may hold values from -6 to 6
- order: int32 [524288], P(('leaf', 'grp')), may hold values from 0 to 1023, as said below
- near_mask: int32 [512, 5], P(('leaf', 'grp')), may hold values from 0 to 1, as said below
- skeletons: int32 [512, 7, 128], P(('leaf', 'grp')), may hold values from 0 to 1023, as said below
- leaf_interp: bfloat16 [128, 524288], P(None, ('leaf', 'grp')), may hold values from -0.5 to 0.5
- transfer: bfloat16 [512, 6, 128, 128], P(('leaf', 'grp')), as said below
Outputs:
- potentials: float32 [64, 524288], P(None, ('leaf', 'grp'))
The draws below stay inside these ranges and needn't reach their ends.
Inputs may be any that keep to these rules, and one draw needn't show every extreme that they name: `order`: within each block of 1024 consecutive entries, a permutation of 0 to 1023. `near_mask`: entry 2 of every row is 1; an entry is 0 where it points outside the leaf coordinates; the pattern is symmetric: block b marks the block k leaf coordinates away exactly when that block marks b. Level 0 holds 128 different rows of the block; level j >= 1 holds 128 different positions of 0 to 255 in the two children's skeletons; the set of a node is the same on every block of that node. `transfer`: the matrix of a node is the same on every block of that node.
All inputs are finite; a program needn't handle non-finite values.
Results may differ from the reference program's by a relative error of at most 0.0019.
Values may be sent and summed in bfloat16 or wider, within the bound.
A program may use at most 64 MiB of HBM per device.

```python
import jax
import jax.numpy as jnp
from jax import lax

DIM = 256
RHS = 64
SK = 128
LEAF = 1024
REACH = 2
LEVELS = 6
BLOCKS = 512
ROWS = 524288
N_LEAF = 64
N_GRP = 8


def draw_points(key, part):
    values = jnp.clip(jax.random.normal(key, (DIM, ROWS), jnp.float32), -6.0, 6.0)
    return values.astype(jnp.bfloat16)


def draw_order(key, part):
    subkeys = jax.random.split(key, BLOCKS)
    shuffled = jax.vmap(lambda subkey: jax.random.permutation(subkey, LEAF))(subkeys)
    return shuffled.reshape(-1).astype(jnp.int32)


def draw_near_mask(key, part):
    coin_flips = jax.random.randint(key, (N_LEAF, N_GRP, REACH), 0, 2, dtype=jnp.int32)
    leaf_coord = jnp.arange(N_LEAF, dtype=jnp.int32)[:, None]
    upward = []
    for distance in range(1, REACH + 1):
        inside = (leaf_coord + distance < N_LEAF).astype(jnp.int32)
        upward.append(coin_flips[:, :, distance - 1] * inside)
    downward = []
    for distance in range(1, REACH + 1):
        moved = jnp.pad(upward[distance - 1], ((distance, 0), (0, 0)))[:N_LEAF]
        downward.append(moved)
    columns = [downward[distance - 1] for distance in range(REACH, 0, -1)]
    columns = columns + [jnp.ones((N_LEAF, N_GRP), jnp.int32)] + upward
    return jnp.stack(columns, axis=2).reshape(BLOCKS, 2 * REACH + 1).astype(jnp.int32)


def draw_skeletons(key, part):
    per_level = []
    for level in range(LEVELS + 1):
        count = (N_LEAF >> level) * N_GRP
        span = LEAF if level == 0 else 2 * SK
        subkeys = jax.random.split(jax.random.fold_in(key, level), count)
        chosen = jax.vmap(lambda subkey: jax.random.permutation(subkey, span)[:SK])(subkeys)
        if level == 0:
            node_ids = jnp.arange(count, dtype=jnp.int32)
            wanted = jnp.where(node_ids == 0, span - 1, 0)
            moved_by = (wanted - chosen[:, 0]) % span
            chosen = jnp.where((node_ids < 2)[:, None], (chosen + moved_by[:, None]) % span, chosen)
        chosen = chosen.reshape(N_LEAF >> level, N_GRP, SK)
        per_level.append(jnp.repeat(chosen, 2 ** level, axis=0))
    return jnp.stack(per_level, axis=2).reshape(BLOCKS, LEVELS + 1, SK).astype(jnp.int32)


def draw_transfer(key, part):
    per_level = []
    for level in range(LEVELS):
        count = N_LEAF >> level
        level_key = jax.random.fold_in(key, 100 + level)
        values = jax.random.normal(level_key, (count, N_GRP, SK, SK), jnp.float32)
        values = values / jnp.sqrt(2.0 * SK)
        per_level.append(jnp.repeat(values, 2 ** level, axis=0))
    return jnp.stack(per_level, axis=2).reshape(BLOCKS, LEVELS, SK, SK).astype(jnp.bfloat16)


def level_of(key, extent, pieces, low, high):
    loudness, own = 1.0, jax.random.fold_in(key, 6)
    for position, blocks in pieces:
        heights = jnp.exp(jax.random.uniform(jax.random.fold_in(own, position), (blocks,), jnp.float32, low / len(pieces), high / len(pieces)))
        loudness = loudness * jnp.repeat(heights, extent[position] // blocks).reshape([-1 if axis == position else 1 for axis in range(len(extent))])
    return loudness


def noise(rng, extent, deviation, bound, shards=(), kind=jnp.bfloat16):
    entries = jax.random.normal(rng, extent, jnp.float32) * deviation
    if len(shards) > 0:
        entries = level_of(rng, extent, shards, -0.22, 0.18) * entries
    return jnp.clip(entries, min=-bound, max=bound).astype(kind)


def setup_inputs(seed: int = 0) -> dict:
    splits = jax.random.split(jax.random.key(seed), 8)
    points = draw_points(jax.random.fold_in(splits[7], 71), 0)
    charges = noise(splits[1], (RHS, ROWS), 1.0, 6.0, ((1, 512),))
    order = draw_order(jax.random.fold_in(splits[7], 71), 0)
    near_mask = draw_near_mask(jax.random.fold_in(splits[7], 71), 0)
    skeletons = draw_skeletons(jax.random.fold_in(splits[7], 71), 0)
    leaf_interp = noise(splits[5], (SK, ROWS), SK ** -0.5, 0.5, ((1, 512),))
    transfer = draw_transfer(jax.random.fold_in(splits[7], 71), 0)
    return dict(points=points, charges=charges, order=order, near_mask=near_mask, skeletons=skeletons, leaf_interp=leaf_interp, transfer=transfer)


def pair_kernel(source, target):
    source_wide = source.astype(jnp.float32)
    target_wide = target.astype(jnp.float32)
    source_square = jnp.sum(source_wide * source_wide, axis=0)
    target_square = jnp.sum(target_wide * target_wide, axis=0)
    inner = jnp.dot(source.T, target, preferred_element_type=jnp.float32)
    return jnp.exp(-2.0 * (source_square[:, None] + target_square[None, :] - 2.0 * inner) / DIM)


def reference(points, charges, order, near_mask, skeletons, leaf_interp, transfer):
    highest = lax.Precision.HIGHEST
    ordered = jnp.take_along_axis(charges.reshape(RHS, BLOCKS, LEAF), order.reshape(1, BLOCKS, LEAF), axis=2).reshape(RHS, BLOCKS * LEAF)

    def near_block(block_id):
        leaf_coord = block_id // N_GRP
        group_id = block_id % N_GRP
        target = lax.dynamic_slice_in_dim(points, block_id * LEAF, LEAF, axis=1)
        running = jnp.zeros((RHS, LEAF), jnp.float32)
        for offset in range(-REACH, REACH + 1):
            neighbour = leaf_coord + offset
            usable = (neighbour >= 0) & (neighbour < N_LEAF) & (near_mask[block_id, offset + REACH] == 1)
            source_id = (jnp.clip(neighbour, 0, N_LEAF - 1) * N_GRP + group_id).astype(jnp.int32)

            def add_tile(carry, source_id=source_id):
                source = lax.dynamic_slice_in_dim(points, source_id * LEAF, LEAF, axis=1)
                source_charges = lax.dynamic_slice_in_dim(ordered, source_id * LEAF, LEAF, axis=1)
                tile = pair_kernel(source, target).astype(jnp.bfloat16)
                return carry + jnp.dot(source_charges, tile, preferred_element_type=jnp.float32)

            running = lax.cond(usable, add_tile, lambda carry: carry, running)
        return running

    near_field = lax.map(near_block, jnp.arange(BLOCKS, dtype=jnp.int32))

    blocked_points = points.reshape(DIM, BLOCKS, LEAF)
    blocked_interp = leaf_interp.reshape(SK, BLOCKS, LEAF).astype(jnp.float32)
    blocked_ordered = ordered.reshape(RHS, BLOCKS, LEAF).astype(jnp.float32)
    weights_now = jnp.einsum("rbl,kbl->brk", blocked_ordered, blocked_interp, precision=highest)
    weights_now = weights_now.reshape(N_LEAF, N_GRP, RHS, SK)
    coords = jnp.take_along_axis(blocked_points, skeletons[:, 0, :][None], axis=2)
    coords = jnp.transpose(coords, (1, 0, 2)).reshape(N_LEAF, N_GRP, DIM, SK)
    skeleton_table = skeletons.reshape(N_LEAF, N_GRP, LEVELS + 1, SK)
    transfer_table = transfer.reshape(N_LEAF, N_GRP, LEVELS, SK, SK)
    history = []
    for level in range(1, LEVELS + 1):
        stride = 2 ** (level - 1)
        matrices = transfer_table[::stride, :, level - 1].astype(jnp.float32)
        contrib = jnp.einsum("lgrk,lgmk->lgrm", weights_now, matrices, precision=highest)
        history.append((weights_now, coords))
        joined = jnp.concatenate([coords[0::2], coords[1::2]], axis=3)
        chosen = skeleton_table[::2 * stride, :, level]
        coords = jnp.take_along_axis(joined, chosen[:, :, None, :], axis=3)
        weights_now = contrib[0::2] + contrib[1::2]

    top_coords = coords[0]
    top_weights = weights_now[0]
    kernels = jax.vmap(lambda source: jax.vmap(lambda target: pair_kernel(source, target))(top_coords))(top_coords)
    keep = (jnp.arange(N_GRP)[:, None] != jnp.arange(N_GRP)[None, :]).astype(jnp.float32)
    potential = jnp.einsum("hrk,hgkm->grm", top_weights, kernels * keep[:, :, None, None], precision=highest)[None]

    for level in range(LEVELS, 0, -1):
        child_weights, child_coords = history[level - 1]
        count = child_weights.shape[0]
        matrices = transfer_table[::2 ** (level - 1), :, level - 1].astype(jnp.float32)
        inherited = jnp.repeat(potential, 2, axis=0)
        sibling_weights = child_weights.reshape(count // 2, 2, N_GRP, RHS, SK)[:, ::-1].reshape(child_weights.shape)
        sibling_coords = child_coords.reshape(count // 2, 2, N_GRP, DIM, SK)[:, ::-1].reshape(child_coords.shape)
        sibling_kernels = jax.vmap(jax.vmap(pair_kernel))(sibling_coords, child_coords)
        potential = jnp.einsum("lgrk,lgkm->lgrm", inherited, matrices, precision=highest) + jnp.einsum("lgrk,lgkm->lgrm", sibling_weights, sibling_kernels, precision=highest)

    far_field = jnp.einsum("brk,kbl->rbl", potential.reshape(BLOCKS, RHS, SK), blocked_interp, precision=highest)
    near_moved = jnp.transpose(near_field, (1, 0, 2))
    return (near_moved + far_field).reshape(RHS, BLOCKS * LEAF)
```

```python
import functools
import math

import jax
import jax.numpy as jnp
from jax import lax
from jax.experimental import pallas as pl
from jax.experimental.pallas import tpu as pltpu
from jax.sharding import PartitionSpec as P

MESH = pl.DeviceIdType.MESH
F32 = jnp.float32
BF16 = jnp.bfloat16
DIM, RHS, SK, LEAF, LEVELS = 256, 64, 128, 1024, 6
HALF_DIM, HALF_RHS = DIM // 2, RHS // 2
CONTRIB, COORD, WEIGHT, BUNDLE = 0, 2 * HALF_RHS, 2 * HALF_RHS + HALF_DIM, 4 * HALF_RHS + HALF_DIM
TOP = HALF_DIM + HALF_RHS
SCALE = 2.0 / DIM / math.log(2.0)
CHUNK = 256


def dot(a, b):
    return jnp.dot(a, b, preferred_element_type=F32)


def dot_nt(a, b):
    return lax.dot_general(a, b, (((1,), (1,)), ((), ())), preferred_element_type=F32)


def split(value):
    high = value.astype(BF16)
    low = (value - high.astype(F32)).astype(BF16)
    return high, low


def pair_kernel(source_t, target):
    wide_s = source_t.astype(F32)
    wide_t = target.astype(F32)
    square_s = jnp.sum(wide_s * wide_s, axis=1, keepdims=True) * SCALE
    square_t = jnp.sum(wide_t * wide_t, axis=0, keepdims=True) * SCALE
    return jnp.exp2(dot(source_t, target) * (2.0 * SCALE) - (square_s + square_t))


def kernel(
    n_y, n_x, n_grp,
    points_hbm, charges_hbm, order_hbm, mask_ref, skel_hbm, interp_hbm, transfer_hbm,
    out_ref,
    pts, chg, order, skel, interp, transfer,
    pts_t, ordered, norm_t, near_pts, near_chg, near,
    own, sib, top, far,
    load_sem, send_sem, recv_sem,
):
    leaf = lax.axis_index("leaf")
    grp = lax.axis_index("grp")
    core = leaf % 2
    other = 1 - core
    chip = leaf // 2
    y = chip % n_y
    x = chip // n_y
    n_chip = n_x * n_y
    has_a = chip > 0
    has_b = chip < n_chip - 1
    quad = y % 4

    def at_yx(yy, xx):
        return ((xx * n_y + (yy + n_y) % n_y) * 2 + core, grp)

    partner = (chip * 2 + other, grp)

    loads = [
        pltpu.make_async_copy(src, dst, load_sem.at[i])
        for i, (src, dst) in enumerate(
            [
                (order_hbm, order),
                (charges_hbm, chg),
                (interp_hbm, interp),
                (skel_hbm, skel),
                (points_hbm, pts),
                (transfer_hbm, transfer),
            ]
        )
    ]
    for load in loads:
        load.start()

    barrier = pltpu.get_barrier_semaphore()
    peers = [
        partner,
        at_yx(y + 1, x),
        at_yx(y - 1, x),
        at_yx(y + 2, x),
        at_yx(y - 2, x),
        at_yx(y, x ^ 1),
        at_yx(y, n_x - 1 - x),
    ]
    for step in range(1, n_grp):
        peers.append((leaf, (grp + step) % n_grp))
    for peer in peers:
        pl.semaphore_signal(barrier, inc=1, device_id=peer, device_id_type=MESH)

    @pl.when(has_a)
    def _():
        pl.semaphore_signal(barrier, inc=1, device_id=(leaf - 2, grp), device_id_type=MESH)

    @pl.when(has_b)
    def _():
        pl.semaphore_signal(barrier, inc=1, device_id=(leaf + 2, grp), device_id_type=MESH)

    def remote(src, dst, send, recv, device):
        return pltpu.make_async_remote_copy(
            src_ref=src,
            dst_ref=dst,
            send_sem=send_sem.at[send],
            recv_sem=recv_sem.at[recv],
            device_id=device,
            device_id_type=MESH,
        )

    loads[0].wait()
    loads[1].wait()
    for column in range(0, LEAF, CHUNK):
        wanted = order[:, column : column + CHUNK]
        rows = lax.broadcasted_iota(jnp.int32, (LEAF, CHUNK), 0)
        pick = jnp.where(rows == wanted, 1.0, 0.0).astype(BF16)
        ordered[:, column : column + CHUNK] = dot(chg[...], pick).astype(BF16)
    loads[2].wait()
    weights = dot_nt(ordered[...], interp[...])
    loads[3].wait()
    loads[4].wait()
    rows = lax.broadcasted_iota(jnp.int32, (LEAF, SK), 0)
    pick = jnp.where(rows == skel[0:1, :], 1.0, 0.0).astype(BF16)
    coords = dot(pts[...], pick).astype(BF16)
    loads[5].wait()

    def contribution(weights, level):
        high, low = split(weights)
        both = dot_nt(jnp.concatenate([high, low], axis=0), transfer[level])
        count = weights.shape[0]
        return high, low, both[:count] + both[count:]

    high, low, contrib = contribution(weights, 0)
    contrib_high, contrib_low = split(contrib)
    for half in range(2):
        part = slice(half * HALF_RHS, (half + 1) * HALF_RHS)
        own[0, half, 0:HALF_RHS] = contrib_high[part]
        own[0, half, HALF_RHS:COORD] = contrib_low[part]
        own[0, half, COORD:WEIGHT] = coords[half * HALF_DIM : (half + 1) * HALF_DIM]
        own[0, half, WEIGHT : WEIGHT + HALF_RHS] = high[part]
        own[0, half, WEIGHT + HALF_RHS : BUNDLE] = low[part]

    expected = len(peers) + has_a.astype(jnp.int32) + has_b.astype(jnp.int32)
    pl.semaphore_wait(barrier, expected)

    first = remote(own.at[0], sib.at[0], 0, 0, partner)
    first.start()
    for row in range(0, LEAF, CHUNK):
        pts_t[row : row + CHUNK, :] = jnp.transpose(pts[:, row : row + CHUNK])
    near_p = [
        remote(pts_t, near_pts.at[0], 1, 1, partner),
        remote(ordered, near_chg.at[0], 2, 2, partner),
    ]
    for copy in near_p:
        copy.start()
    wide = pts[...].astype(F32)
    norm_t[...] = jnp.sum(wide * wide, axis=0, keepdims=True) * SCALE
    near[...] = jnp.zeros_like(near)

    def near_tile(source_t, source_chg, keep):
        def body(step, carry):
            rows = pl.ds(pl.multiple_of(step * CHUNK, CHUNK), CHUNK)
            lhs = source_t[rows, :]
            wide = lhs.astype(F32)
            norm_s = jnp.sum(wide * wide, axis=1, keepdims=True) * SCALE
            charge = source_chg[:, rows]
            if keep is not None:
                charge = jnp.where(keep > 0, charge, jnp.zeros_like(charge))
            inner = dot(lhs, pts[...])
            tile = jnp.exp2(inner * (2.0 * SCALE) - (norm_s + norm_t[...])).astype(BF16)
            near[...] += dot(charge, tile)
            return carry

        lax.fori_loop(0, LEAF // CHUNK, body, 0)

    bits = [core, y % 2, (y // 2) % 2, (y // 4) % 2, x % 2, (x // 2) % 2]

    def selection(level):
        wanted = skel[level + 1 : level + 2, :]
        rows = lax.broadcasted_iota(jnp.int32, (SK, SK), 0)
        upper = bits[level] * SK
        mine = jnp.where(rows + upper == wanted, 1.0, 0.0).astype(BF16)
        theirs = jnp.where(rows + (SK - upper) == wanted, 1.0, 0.0).astype(BF16)
        return mine, theirs

    def joined_coords(level, half, picks):
        mine, theirs = picks
        picked = dot(own[level, half, COORD:WEIGHT, :], mine) + dot(
            sib[level, half, COORD:WEIGHT, :], theirs
        )
        return picked.astype(BF16)

    def summed_weights(level, half):
        total = own[level, half, 0:HALF_RHS].astype(F32) + own[
            level, half, HALF_RHS:COORD
        ].astype(F32)
        return (
            total
            + sib[level, half, 0:HALF_RHS].astype(F32)
            + sib[level, half, HALF_RHS:COORD].astype(F32)
        )

    def raise_level(level):
        own[level + 1, core, COORD:WEIGHT] = joined_coords(level, core, selection(level))
        weights = summed_weights(level, core)
        if level + 1 < LEVELS:
            high, low, contrib = contribution(weights, level + 1)
            contrib_high, contrib_low = split(contrib)
            own[level + 1, core, 0:HALF_RHS] = contrib_high
            own[level + 1, core, HALF_RHS:COORD] = contrib_low
            own[level + 1, core, WEIGHT : WEIGHT + HALF_RHS] = high
            own[level + 1, core, WEIGHT + HALF_RHS : BUNDLE] = low
        else:
            own[level + 1, core, WEIGHT : WEIGHT + HALF_RHS] = weights.astype(BF16)

    def raise_rest(level):
        own[level + 1, other, COORD:WEIGHT] = joined_coords(level, other, selection(level))

    def sibling_field(level):
        source = jnp.concatenate(
            [sib[level, 0, COORD:WEIGHT, :], sib[level, 1, COORD:WEIGHT, :]], axis=0
        )
        target = jnp.concatenate(
            [own[level, 0, COORD:WEIGHT, :], own[level, 1, COORD:WEIGHT, :]], axis=0
        )
        kern_high, kern_low = split(pair_kernel(jnp.transpose(source), target))
        high = jnp.concatenate(
            [sib[level, half, WEIGHT : WEIGHT + HALF_RHS, :] for half in range(2)], axis=0
        )
        low = jnp.concatenate(
            [sib[level, half, WEIGHT + HALF_RHS : BUNDLE, :] for half in range(2)], axis=0
        )
        both = dot(jnp.concatenate([high, low], axis=0), kern_high)
        far[level] = both[:RHS] + both[RHS:] + dot(high, kern_low)

    routes = {
        1: [(None, at_yx(y ^ 1, x))],
        2: [
            (quad == 1, at_yx(y + 2, x)),
            (quad == 1, at_yx(y + 1, x)),
            (quad == 2, at_yx(y - 2, x)),
            (quad == 2, at_yx(y - 1, x)),
        ],
        3: [
            (quad == 3, at_yx(y + 2, x)),
            (quad == 3, at_yx(y + 1, x)),
            (quad == 0, at_yx(y - 2, x)),
            (quad == 0, at_yx(y - 1, x)),
        ],
        4: [(None, at_yx(y, x ^ 1))],
        5: [(None, at_yx(y, n_x - 1 - x))],
    }

    def when(condition, action):
        if condition is None:
            action()
        else:
            pl.when(condition)(action)

    def bundle_copies(level):
        main, rest = [], []
        for index, (condition, device) in enumerate(routes[level]):
            base = 3 + (level - 1) * 8 + (index % 2) * 2
            recv = 3 + (level - 1) * 2
            source, target = own.at[level, core], sib.at[level, core]
            main.append(
                (
                    condition,
                    remote(
                        source.at[pl.ds(0, WEIGHT), :],
                        target.at[pl.ds(0, WEIGHT), :],
                        base,
                        recv,
                        device,
                    ),
                )
            )
            rest.append(
                (
                    condition,
                    remote(
                        source.at[pl.ds(WEIGHT, 2 * HALF_RHS), :],
                        target.at[pl.ds(WEIGHT, 2 * HALF_RHS), :],
                        base + 1,
                        recv + 1,
                        device,
                    ),
                )
            )
        return main, rest

    copies = {level: bundle_copies(level) for level in routes}

    def forward(level):
        part = pl.ds(COORD, BUNDLE - COORD)
        return remote(
            sib.at[level, core].at[part, :],
            sib.at[level, core].at[part, :],
            43 + level,
            13 + level,
            partner,
        )

    def forwarded(level):
        part = pl.ds(COORD, BUNDLE - COORD)
        return remote(
            sib.at[level, other].at[part, :],
            sib.at[level, other].at[part, :],
            43 + level,
            13 + level,
            partner,
        )

    def send_level(level):
        for condition, copy in copies[level][0] + copies[level][1]:
            when(condition, copy.start)

    def finish_sends(level):
        for condition, copy in copies[level][0] + copies[level][1]:
            when(condition, copy.wait_send)

    first.wait_recv()
    raise_level(0)
    send_level(1)
    raise_rest(0)
    sibling_field(0)

    near_tile(pts_t, ordered, None)

    def receive_main(level):
        copies[level][0][0][1].wait_recv()

    def receive_rest(level):
        copies[level][1][0][1].wait_recv()
        forward(level).start()

    receive_main(1)
    raise_level(1)
    send_level(2)
    receive_rest(1)

    keep_p = jnp.where(core == 0, mask_ref[0, 3], mask_ref[0, 1])
    keep_f = jnp.where(core == 0, mask_ref[0, 1], mask_ref[0, 3])
    for copy in near_p:
        copy.wait_recv()
    near_tile(near_pts.at[0], near_chg.at[0], keep_p)
    forwarded(1).wait_recv()
    raise_rest(1)

    receive_main(2)
    raise_level(2)
    send_level(3)
    receive_rest(2)
    sibling_field(1)
    forwarded(2).wait_recv()
    raise_rest(2)
    sibling_field(2)

    receive_main(3)
    raise_level(3)
    send_level(4)
    receive_rest(3)

    near_a = [
        remote(pts_t, near_pts.at[1], 49, 19, (leaf + 2, grp)),
        remote(ordered, near_chg.at[1], 50, 20, (leaf + 2, grp)),
    ]
    near_b = [
        remote(pts_t, near_pts.at[2], 51, 21, (leaf - 2, grp)),
        remote(ordered, near_chg.at[2], 52, 22, (leaf - 2, grp)),
    ]

    @pl.when(has_b)
    def _():
        for copy in near_a:
            copy.start()

    @pl.when(has_a)
    def _():
        for copy in near_b:
            copy.start()

    forwarded(3).wait_recv()
    raise_rest(3)
    sibling_field(3)

    receive_main(4)
    raise_level(4)
    send_level(5)
    receive_rest(4)
    forwarded(4).wait_recv()
    raise_rest(4)
    sibling_field(4)

    receive_main(5)
    raise_level(5)

    message = pl.ds(COORD, TOP)
    top_copies = []
    for step in sorted(range(1, n_grp), key=lambda d: -min(d, n_grp - d)):
        copy = remote(
            own.at[LEVELS, core].at[message, :],
            top.at[step - 1, core],
            53 + step,
            23 + step,
            (leaf, (grp + step) % n_grp),
        )
        copy.start()
        top_copies.append((step, copy))

    receive_rest(5)
    forwarded(5).wait_recv()
    raise_rest(5)
    sibling_field(5)

    pass_on_a = [
        remote(near_pts.at[1], near_pts.at[3], 68, 38, partner),
        remote(near_chg.at[1], near_chg.at[3], 69, 39, partner),
    ]
    pass_on_b = [
        remote(near_pts.at[2], near_pts.at[3], 68, 38, partner),
        remote(near_chg.at[2], near_chg.at[3], 69, 39, partner),
    ]

    @pl.when(has_a)
    def _():
        for copy in near_a:
            copy.wait_recv()

        @pl.when(core == 1)
        def _():
            for copy in pass_on_a:
                copy.start()

    @pl.when(has_b)
    def _():
        for copy in near_b:
            copy.wait_recv()

        @pl.when(core == 0)
        def _():
            for copy in pass_on_b:
                copy.start()

    def top_forward(step, half):
        return remote(
            top.at[step - 1, half], top.at[step - 1, half], 60 + step, 30 + step, partner
        )

    @pl.when(has_a)
    def _():
        near_tile(near_pts.at[1], near_chg.at[1], mask_ref[0, 0])

    for step, copy in reversed(top_copies):
        copy.wait_recv()
        top_forward(step, core).start()

    @pl.when(has_b)
    def _():
        near_tile(near_pts.at[2], near_chg.at[2], mask_ref[0, 4])

    has_f = jnp.logical_or(
        jnp.logical_and(core == 0, has_a), jnp.logical_and(core == 1, has_b)
    )

    @pl.when(has_f)
    def _():
        for copy in pass_on_a:
            copy.wait_recv()
        near_tile(near_pts.at[3], near_chg.at[3], keep_f)

    target = jnp.concatenate(
        [own[LEVELS, 0, COORD:WEIGHT, :], own[LEVELS, 1, COORD:WEIGHT, :]], axis=0
    )
    potential = jnp.zeros((RHS, SK), F32)
    for step, _ in reversed(top_copies):
        top_forward(step, other).wait_recv()
        source = jnp.concatenate([top[step - 1, half, 0:HALF_DIM, :] for half in range(2)], axis=0)
        kern_high, kern_low = split(pair_kernel(jnp.transpose(source), target))
        high = jnp.concatenate(
            [top[step - 1, half, HALF_DIM:TOP, :] for half in range(2)], axis=0
        )
        potential = potential + dot(high, kern_high) + dot(high, kern_low)

    def times(value, matrix):
        high, low = split(value)
        both = dot(jnp.concatenate([high, low], axis=0), matrix)
        return both[:RHS] + both[RHS:]

    for level in range(LEVELS - 1, -1, -1):
        potential = times(potential, transfer[level]) + far[level]
    out_ref[...] = near[...] + times(potential, interp[...])

    first.wait_send()
    for copy in near_p:
        copy.wait_send()
    for level in routes:
        finish_sends(level)
        forward(level).wait_send()

    @pl.when(has_b)
    def _():
        for copy in near_a:
            copy.wait_send()

        @pl.when(core == 0)
        def _():
            for copy in pass_on_b:
                copy.wait_send()

    @pl.when(has_a)
    def _():
        for copy in near_b:
            copy.wait_send()

        @pl.when(core == 1)
        def _():
            for copy in pass_on_a:
                copy.wait_send()

    for step, copy in top_copies:
        copy.wait_send()
        top_forward(step, core).wait_send()


def solution(mesh):
    n_grp = mesh.shape["grp"]
    n_x, n_y = 4, mesh.shape["leaf"] // 8
    vmem = pltpu.VMEM

    def local(points, charges, order, near_mask, skeletons, leaf_interp, transfer):
        anywhere = pl.BlockSpec(memory_space=pl.ANY)
        return pl.pallas_call(
            functools.partial(kernel, n_y, n_x, n_grp),
            out_shape=jax.ShapeDtypeStruct((RHS, LEAF), F32),
            in_specs=[anywhere] * 3 + [pl.BlockSpec(memory_space=pltpu.SMEM)] + [anywhere] * 3,
            out_specs=pl.BlockSpec(memory_space=pltpu.VMEM),
            scratch_shapes=[
                vmem((DIM, LEAF), BF16),
                vmem((RHS, LEAF), BF16),
                vmem((1, LEAF), jnp.int32),
                vmem((LEVELS + 1, SK), jnp.int32),
                vmem((SK, LEAF), BF16),
                vmem((LEVELS, SK, SK), BF16),
                vmem((LEAF, DIM), BF16),
                vmem((RHS, LEAF), BF16),
                vmem((1, LEAF), F32),
                vmem((4, LEAF, DIM), BF16),
                vmem((4, RHS, LEAF), BF16),
                vmem((RHS, LEAF), F32),
                vmem((LEVELS + 1, 2, BUNDLE, SK), BF16),
                vmem((LEVELS, 2, BUNDLE, SK), BF16),
                vmem((n_grp - 1, 2, TOP, SK), BF16),
                vmem((LEVELS, RHS, SK), F32),
                pltpu.SemaphoreType.DMA((6,)),
                pltpu.SemaphoreType.DMA((70,)),
                pltpu.SemaphoreType.DMA((40,)),
            ],
            compiler_params=pltpu.CompilerParams(
                collective_id=0, has_side_effects=True, vmem_limit_bytes=48 * 1024 * 1024
            ),
        )(
            points,
            charges,
            order.reshape(1, LEAF),
            near_mask,
            skeletons.reshape(LEVELS + 1, SK),
            leaf_interp,
            transfer.reshape(LEVELS, SK, SK),
        )

    in_specs = (
        P(None, ("leaf", "grp")),
        P(None, ("leaf", "grp")),
        P(("leaf", "grp")),
        P(("leaf", "grp"), None),
        P(("leaf", "grp"), None, None),
        P(None, ("leaf", "grp")),
        P(("leaf", "grp"), None, None, None),
    )
    out_specs = P(None, ("leaf", "grp"))
    return jax.shard_map(local, mesh=mesh, in_specs=in_specs, out_specs=out_specs, check_vma=False)
```

```python
import functools
import math

import jax
import jax.numpy as jnp
from jax import lax
from jax.experimental import pallas as pl
from jax.experimental.pallas import tpu as pltpu
from jax.sharding import PartitionSpec as P

MESH = pl.DeviceIdType.MESH
F32 = jnp.float32
BF16 = jnp.bfloat16
DIM, RHS, SK, LEAF, LEVELS = 256, 64, 128, 1024, 6
HALF_DIM, HALF_RHS = DIM // 2, RHS // 2
CONTRIB, COORD, WEIGHT, BUNDLE = 0, 2 * HALF_RHS, 2 * HALF_RHS + HALF_DIM, 4 * HALF_RHS + HALF_DIM
TOP = HALF_DIM + HALF_RHS
SCALE = 2.0 / DIM / math.log(2.0)
CHUNK = 256
N_PIECE = 10


def dot(a, b):
    return jnp.dot(a, b, preferred_element_type=F32)


def dot_nt(a, b):
    return lax.dot_general(a, b, (((1,), (1,)), ((), ())), preferred_element_type=F32)


def split(value):
    high = value.astype(BF16)
    low = (value - high.astype(F32)).astype(BF16)
    return high, low


def pair_kernel(source_t, target):
    wide_s = source_t.astype(F32)
    wide_t = target.astype(F32)
    square_s = jnp.sum(wide_s * wide_s, axis=1, keepdims=True) * SCALE
    square_t = jnp.sum(wide_t * wide_t, axis=0, keepdims=True) * SCALE
    return jnp.exp2(dot(source_t, target) * (2.0 * SCALE) - (square_s + square_t))


def kernel(
    n_y, n_x, n_grp,
    points_hbm, charges_hbm, order_hbm, mask_ref, skel_hbm, interp_hbm, transfer_hbm,
    out_ref,
    pts, chg, order, skel, interp, transfer,
    pts_t, ordered, norm_t, near_pts, near_chg, near,
    own, sib, top, far,
    load_sem, send_sem, recv_sem,
):
    leaf = lax.axis_index("leaf")
    grp = lax.axis_index("grp")
    core = leaf % 2
    other = 1 - core
    chip = leaf // 2
    y = chip % n_y
    x = chip // n_y
    n_chip = n_x * n_y
    has_a = chip > 0
    has_b = chip < n_chip - 1
    quad = y % 4

    def at_yx(yy, xx):
        return ((xx * n_y + (yy + n_y) % n_y) * 2 + core, grp)

    partner = (chip * 2 + other, grp)

    loads = [
        pltpu.make_async_copy(src, dst, load_sem.at[i])
        for i, (src, dst) in enumerate(
            [
                (order_hbm, order),
                (charges_hbm, chg),
                (interp_hbm, interp),
                (skel_hbm, skel),
                (points_hbm, pts),
                (transfer_hbm, transfer),
            ]
        )
    ]
    for load in loads:
        load.start()

    barrier = pltpu.get_barrier_semaphore()
    peers = [
        partner,
        at_yx(y + 1, x),
        at_yx(y - 1, x),
        at_yx(y + 2, x),
        at_yx(y - 2, x),
        at_yx(y, x ^ 1),
        at_yx(y, n_x - 1 - x),
    ]
    for step in range(1, n_grp):
        peers.append((leaf, (grp + step) % n_grp))
    for peer in peers:
        pl.semaphore_signal(barrier, inc=1, device_id=peer, device_id_type=MESH)

    @pl.when(has_a)
    def _():
        pl.semaphore_signal(barrier, inc=1, device_id=(leaf - 2, grp), device_id_type=MESH)

    @pl.when(has_b)
    def _():
        pl.semaphore_signal(barrier, inc=1, device_id=(leaf + 2, grp), device_id_type=MESH)

    def remote(src, dst, send, recv, device):
        return pltpu.make_async_remote_copy(
            src_ref=src,
            dst_ref=dst,
            send_sem=send_sem.at[send],
            recv_sem=recv_sem.at[recv],
            device_id=device,
            device_id_type=MESH,
        )

    loads[0].wait()
    loads[1].wait()
    for column in range(0, LEAF, CHUNK):
        wanted = order[:, column : column + CHUNK]
        rows = lax.broadcasted_iota(jnp.int32, (LEAF, CHUNK), 0)
        pick = jnp.where(rows == wanted, 1.0, 0.0).astype(BF16)
        ordered[:, column : column + CHUNK] = dot(chg[...], pick).astype(BF16)
    loads[2].wait()
    weights = dot_nt(ordered[...], interp[...])
    loads[3].wait()
    loads[4].wait()
    rows = lax.broadcasted_iota(jnp.int32, (LEAF, SK), 0)
    pick = jnp.where(rows == skel[0], 1.0, 0.0).astype(BF16)
    coords = dot(pts[...], pick).astype(BF16)
    loads[5].wait()

    def contribution(weights, level):
        high, low = split(weights)
        both = dot_nt(jnp.concatenate([high, low], axis=0), transfer[level])
        count = weights.shape[0]
        return high, low, both[:count] + both[count:]

    high, low, contrib = contribution(weights, 0)
    contrib_high, contrib_low = split(contrib)
    for half in range(2):
        part = slice(half * HALF_RHS, (half + 1) * HALF_RHS)
        own[0, half, 0:HALF_RHS] = contrib_high[part]
        own[0, half, HALF_RHS:COORD] = contrib_low[part]
        own[0, half, COORD:WEIGHT] = coords[half * HALF_DIM : (half + 1) * HALF_DIM]
        own[0, half, WEIGHT : WEIGHT + HALF_RHS] = high[part]
        own[0, half, WEIGHT + HALF_RHS : BUNDLE] = low[part]

    expected = len(peers) + has_a.astype(jnp.int32) + has_b.astype(jnp.int32)
    pl.semaphore_wait(barrier, expected)

    first = remote(own.at[0], sib.at[0], 0, 0, partner)
    first.start()
    for row in range(0, LEAF, CHUNK):
        pts_t[row : row + CHUNK, :] = jnp.transpose(pts[:, row : row + CHUNK])
    near_p = [
        remote(pts_t, near_pts.at[0], 1, 1, partner),
        remote(ordered, near_chg.at[0], 2, 2, partner),
    ]
    for copy in near_p:
        copy.start()
    wide = pts[...].astype(F32)
    norm_t[...] = jnp.sum(wide * wide, axis=0, keepdims=True) * SCALE
    near[...] = jnp.zeros_like(near)

    def near_tile(source_t, source_chg, keep):
        def body(step, carry):
            rows = pl.ds(pl.multiple_of(step * CHUNK, CHUNK), CHUNK)
            lhs = source_t[rows, :]
            wide = lhs.astype(F32)
            norm_s = jnp.sum(wide * wide, axis=1, keepdims=True) * SCALE
            charge = source_chg[:, rows]
            if keep is not None:
                charge = jnp.where(keep > 0, charge, jnp.zeros_like(charge))
            inner = dot(lhs, pts[...])
            tile = jnp.exp2(inner * (2.0 * SCALE) - (norm_s + norm_t[...])).astype(BF16)
            near[...] += dot(charge, tile)
            return carry

        lax.fori_loop(0, LEAF // CHUNK, body, 0)

    bits = [core, y % 2, (y // 2) % 2, (y // 4) % 2, x % 2, (x // 2) % 2]

    def selection(level):
        wanted = skel[level + 1]
        rows = lax.broadcasted_iota(jnp.int32, (SK, SK), 0)
        upper = bits[level] * SK
        mine = jnp.where(rows + upper == wanted, 1.0, 0.0).astype(BF16)
        theirs = jnp.where(rows + (SK - upper) == wanted, 1.0, 0.0).astype(BF16)
        return mine, theirs

    def joined_coords(level, half, picks):
        mine, theirs = picks
        picked = dot(own[level, half, COORD:WEIGHT, :], mine) + dot(
            sib[level, half, COORD:WEIGHT, :], theirs
        )
        return picked.astype(BF16)

    def summed_weights(level, half):
        total = own[level, half, 0:HALF_RHS].astype(F32) + own[
            level, half, HALF_RHS:COORD
        ].astype(F32)
        return (
            total
            + sib[level, half, 0:HALF_RHS].astype(F32)
            + sib[level, half, HALF_RHS:COORD].astype(F32)
        )

    def raise_level(level):
        own[level + 1, core, COORD:WEIGHT] = joined_coords(level, core, selection(level))
        weights = summed_weights(level, core)
        if level + 1 < LEVELS:
            high, low, contrib = contribution(weights, level + 1)
            contrib_high, contrib_low = split(contrib)
            own[level + 1, core, 0:HALF_RHS] = contrib_high
            own[level + 1, core, HALF_RHS:COORD] = contrib_low
            own[level + 1, core, WEIGHT : WEIGHT + HALF_RHS] = high
            own[level + 1, core, WEIGHT + HALF_RHS : BUNDLE] = low
        else:
            own[level + 1, core, WEIGHT : WEIGHT + HALF_RHS] = weights.astype(BF16)

    def raise_rest(level):
        own[level + 1, other, COORD:WEIGHT] = joined_coords(level, other, selection(level))

    def sibling_field(level):
        source = jnp.concatenate(
            [sib[level, 0, COORD:WEIGHT, :], sib[level, 1, COORD:WEIGHT, :]], axis=0
        )
        target = jnp.concatenate(
            [own[level, 0, COORD:WEIGHT, :], own[level, 1, COORD:WEIGHT, :]], axis=0
        )
        kern_high, kern_low = split(pair_kernel(jnp.transpose(source), target))
        high = jnp.concatenate(
            [sib[level, half, WEIGHT : WEIGHT + HALF_RHS, :] for half in range(2)], axis=0
        )
        low = jnp.concatenate(
            [sib[level, half, WEIGHT + HALF_RHS : BUNDLE, :] for half in range(2)], axis=0
        )
        both = dot(jnp.concatenate([high, low], axis=0), kern_high)
        far[level] = both[:RHS] + both[RHS:] + dot(high, kern_low)

    routes = {
        1: [(None, at_yx(y ^ 1, x))],
        2: [
            (quad == 1, at_yx(y + 2, x)),
            (quad == 1, at_yx(y + 1, x)),
            (quad == 2, at_yx(y - 2, x)),
            (quad == 2, at_yx(y - 1, x)),
        ],
        3: [
            (quad == 3, at_yx(y + 2, x)),
            (quad == 3, at_yx(y + 1, x)),
            (quad == 0, at_yx(y - 2, x)),
            (quad == 0, at_yx(y - 1, x)),
        ],
        4: [(None, at_yx(y, x ^ 1))],
        5: [(None, at_yx(y, n_x - 1 - x))],
    }

    def when(condition, action):
        if condition is None:
            action()
        else:
            pl.when(condition)(action)

    def bundle_copies(level):
        main, rest = [], []
        for index, (condition, device) in enumerate(routes[level]):
            base = 3 + (level - 1) * 8 + (index % 2) * 2
            recv = 3 + (level - 1) * 2
            source, target = own.at[level, core], sib.at[level, core]
            main.append(
                (
                    condition,
                    remote(
                        source.at[pl.ds(0, WEIGHT), :],
                        target.at[pl.ds(0, WEIGHT), :],
                        base,
                        recv,
                        device,
                    ),
                )
            )
            rest.append(
                (
                    condition,
                    remote(
                        source.at[pl.ds(WEIGHT, 2 * HALF_RHS), :],
                        target.at[pl.ds(WEIGHT, 2 * HALF_RHS), :],
                        base + 1,
                        recv + 1,
                        device,
                    ),
                )
            )
        return main, rest

    copies = {level: bundle_copies(level) for level in routes}

    def forward(level):
        part = pl.ds(COORD, BUNDLE - COORD)
        return remote(
            sib.at[level, core].at[part, :],
            sib.at[level, core].at[part, :],
            43 + level,
            13 + level,
            partner,
        )

    def forwarded(level):
        part = pl.ds(COORD, BUNDLE - COORD)
        return remote(
            sib.at[level, other].at[part, :],
            sib.at[level, other].at[part, :],
            43 + level,
            13 + level,
            partner,
        )

    sent = []
    due = {}

    def start(copy, condition=None):
        when(condition, copy.start)
        sent.append((condition, copy))

    def expect(name, copy, condition=None):
        due[name] = (condition, copy)

    def arrive(name):
        condition, copy = due.pop(name)
        when(condition, copy.wait_recv)

    def finish():
        for name in list(due):
            arrive(name)
        for condition, copy in sent:
            when(condition, copy.wait_send)

    def send_level(level):
        for condition, copy in copies[level][0] + copies[level][1]:
            start(copy, condition)
        expect(("main", level), copies[level][0][0][1])
        expect(("rest", level), copies[level][1][0][1])

    def receive_main(level):
        arrive(("main", level))

    def receive_rest(level):
        arrive(("rest", level))
        start(forward(level))
        expect(("forward", level), forwarded(level))

    piece_rows = LEAF // (N_PIECE - 2)
    near_a, near_b = [], []
    for slot, shift, there, group in ((1, 2, has_b, near_a), (2, -2, has_a, near_b)):
        for index in range(N_PIECE):
            if index < 2:
                part = pl.ds(index * (RHS // 2), RHS // 2)
                source, target = ordered.at[part, :], near_chg.at[slot, part, :]
            else:
                part = pl.ds((index - 2) * piece_rows, piece_rows)
                source, target = pts_t.at[part, :], near_pts.at[slot, part, :]
            group.append(
                remote(
                    source,
                    target,
                    70 + (slot - 1) * N_PIECE + index,
                    40 + (slot - 1) * N_PIECE + index,
                    (leaf + shift, grp),
                )
            )
    pieces_sent = []

    def send_pieces(count):
        for _ in range(count):
            index = len(pieces_sent)
            pieces_sent.append(index)
            start(near_a[index], has_b)
            start(near_b[index], has_a)
            expect(("a", index), near_a[index], has_a)
            expect(("b", index), near_b[index], has_b)

    sent.append((None, first))
    sent.extend((None, copy) for copy in near_p)
    expect("first", first)
    expect("p0", near_p[0])
    expect("p1", near_p[1])
    send_pieces(2)
    arrive("first")
    raise_level(0)
    send_level(1)
    send_pieces(2)
    raise_rest(0)
    sibling_field(0)

    near_tile(pts_t, ordered, None)

    receive_main(1)
    raise_level(1)
    send_level(2)
    send_pieces(2)
    receive_rest(1)

    keep_p = jnp.where(core == 0, mask_ref[0, 3], mask_ref[0, 1])
    keep_f = jnp.where(core == 0, mask_ref[0, 1], mask_ref[0, 3])
    arrive("p0")
    arrive("p1")
    near_tile(near_pts.at[0], near_chg.at[0], keep_p)
    arrive(("forward", 1))
    raise_rest(1)

    receive_main(2)
    raise_level(2)
    send_level(3)
    send_pieces(2)
    receive_rest(2)
    sibling_field(1)
    arrive(("forward", 2))
    raise_rest(2)
    sibling_field(2)

    receive_main(3)
    raise_level(3)
    send_level(4)
    receive_rest(3)

    send_pieces(2)
    arrive(("forward", 3))
    raise_rest(3)
    sibling_field(3)

    receive_main(4)
    raise_level(4)
    send_level(5)
    receive_rest(4)
    arrive(("forward", 4))
    raise_rest(4)
    sibling_field(4)

    receive_main(5)
    raise_level(5)

    message = pl.ds(COORD, TOP)
    top_copies = []
    for step in sorted(range(1, n_grp), key=lambda d: -min(d, n_grp - d)):
        copy = remote(
            own.at[LEVELS, core].at[message, :],
            top.at[step - 1, core],
            53 + step,
            23 + step,
            (leaf, (grp + step) % n_grp),
        )
        start(copy)
        expect(("top", step), copy)
        top_copies.append((step, copy))

    receive_rest(5)
    arrive(("forward", 5))
    raise_rest(5)
    sibling_field(5)

    pass_on_a = [
        remote(near_pts.at[1], near_pts.at[3], 68, 38, partner),
        remote(near_chg.at[1], near_chg.at[3], 69, 39, partner),
    ]
    pass_on_b = [
        remote(near_pts.at[2], near_pts.at[3], 68, 38, partner),
        remote(near_chg.at[2], near_chg.at[3], 69, 39, partner),
    ]

    has_f = jnp.logical_or(
        jnp.logical_and(core == 0, has_a), jnp.logical_and(core == 1, has_b)
    )
    for index in range(N_PIECE):
        arrive(("a", index))
        arrive(("b", index))
    for index in range(2):
        start(pass_on_a[index], jnp.logical_and(core == 1, has_a))
        start(pass_on_b[index], jnp.logical_and(core == 0, has_b))
        expect(("f", index), pass_on_a[index], has_f)

    def top_forward(step, half):
        return remote(
            top.at[step - 1, half], top.at[step - 1, half], 60 + step, 30 + step, partner
        )

    @pl.when(has_a)
    def _():
        near_tile(near_pts.at[1], near_chg.at[1], mask_ref[0, 0])

    for step, copy in reversed(top_copies):
        arrive(("top", step))
        start(top_forward(step, core))
        expect(("top forward", step), top_forward(step, other))

    @pl.when(has_b)
    def _():
        near_tile(near_pts.at[2], near_chg.at[2], mask_ref[0, 4])

    arrive(("f", 0))
    arrive(("f", 1))

    @pl.when(has_f)
    def _():
        near_tile(near_pts.at[3], near_chg.at[3], keep_f)

    target = jnp.concatenate(
        [own[LEVELS, 0, COORD:WEIGHT, :], own[LEVELS, 1, COORD:WEIGHT, :]], axis=0
    )
    potential = jnp.zeros((RHS, SK), F32)
    for step, _ in reversed(top_copies):
        arrive(("top forward", step))
        source = jnp.concatenate([top[step - 1, half, 0:HALF_DIM, :] for half in range(2)], axis=0)
        kern_high, kern_low = split(pair_kernel(jnp.transpose(source), target))
        high = jnp.concatenate(
            [top[step - 1, half, HALF_DIM:TOP, :] for half in range(2)], axis=0
        )
        potential = potential + dot(high, kern_high) + dot(high, kern_low)

    def times(value, matrix):
        high, low = split(value)
        both = dot(jnp.concatenate([high, low], axis=0), matrix)
        return both[:RHS] + both[RHS:]

    for level in range(LEVELS - 1, -1, -1):
        potential = times(potential, transfer[level]) + far[level]
    out_ref[...] = near[...] + times(potential, interp[...])

    finish()


def solution(mesh):
    n_grp = mesh.shape["grp"]
    n_x, n_y = 4, mesh.shape["leaf"] // 8
    vmem = pltpu.VMEM

    def local(points, charges, order, near_mask, skeletons, leaf_interp, transfer):
        anywhere = pl.BlockSpec(memory_space=pltpu.HBM)
        return pl.pallas_call(
            functools.partial(kernel, n_y, n_x, n_grp),
            out_shape=jax.ShapeDtypeStruct((RHS, LEAF), F32),
            in_specs=[anywhere] * 3 + [pl.BlockSpec(memory_space=pltpu.SMEM)] + [anywhere] * 3,
            out_specs=pl.BlockSpec(memory_space=pltpu.VMEM),
            scratch_shapes=[
                vmem((DIM, LEAF), BF16),
                vmem((RHS, LEAF), BF16),
                vmem((1, LEAF), jnp.int32),
                vmem((LEVELS + 1, 1, SK), jnp.int32),
                vmem((SK, LEAF), BF16),
                vmem((LEVELS, SK, SK), BF16),
                vmem((LEAF, DIM), BF16),
                vmem((RHS, LEAF), BF16),
                vmem((1, LEAF), F32),
                vmem((4, LEAF, DIM), BF16),
                vmem((4, RHS, LEAF), BF16),
                vmem((RHS, LEAF), F32),
                vmem((LEVELS + 1, 2, BUNDLE, SK), BF16),
                vmem((LEVELS, 2, BUNDLE, SK), BF16),
                vmem((n_grp - 1, 2, TOP, SK), BF16),
                vmem((LEVELS, RHS, SK), F32),
                pltpu.SemaphoreType.DMA((6,)),
                pltpu.SemaphoreType.DMA((70 + 2 * N_PIECE,)),
                pltpu.SemaphoreType.DMA((40 + 2 * N_PIECE,)),
            ],
            compiler_params=pltpu.CompilerParams(
                collective_id=0, has_side_effects=True, vmem_limit_bytes=67_043_328
            ),
        )(
            points,
            charges,
            order.reshape(1, LEAF),
            near_mask,
            jnp.transpose(skeletons, (1, 0, 2)),
            leaf_interp,
            transfer.reshape(LEVELS, SK, SK),
        )

    in_specs = (
        P(None, ("leaf", "grp")),
        P(None, ("leaf", "grp")),
        P(("leaf", "grp")),
        P(("leaf", "grp"), None),
        P(("leaf", "grp"), None, None),
        P(None, ("leaf", "grp")),
        P(("leaf", "grp"), None, None, None),
    )
    out_specs = P(None, ("leaf", "grp"))
    return jax.shard_map(local, mesh=mesh, in_specs=in_specs, out_specs=out_specs, check_vma=False)
```

```python
import functools
import itertools
import math

import jax
import jax.numpy as jnp
from jax import lax
from jax.experimental import pallas as pl
from jax.experimental.pallas import tpu as pltpu
from jax.sharding import PartitionSpec as P

MESH = pl.DeviceIdType.MESH
F32 = jnp.float32
BF16 = jnp.bfloat16
DIM, RHS, SK, LEAF, LEVELS = 256, 64, 128, 1024, 6
PART_DIM, PART_RHS = DIM // 4, RHS // 4
COORD = 2 * PART_RHS
WEIGHT = COORD + PART_DIM
LOW = WEIGHT + PART_RHS
BUNDLE = LOW + PART_RHS
TOP = PART_DIM + PART_RHS
SCALE = 2.0 / DIM / math.log(2.0)
CHUNK = 256
N_PIECE = 10
PIECES = (2, 3, 3, 2, 0)


def dot(a, b):
    return jnp.dot(a, b, preferred_element_type=F32)


def dot_nt(a, b):
    return lax.dot_general(a, b, (((1,), (1,)), ((), ())), preferred_element_type=F32)


def split(value):
    high = value.astype(BF16)
    low = (value - high.astype(F32)).astype(BF16)
    return high, low


def pair_kernel(source_t, target):
    wide_s = source_t.astype(F32)
    wide_t = target.astype(F32)
    square_s = jnp.sum(wide_s * wide_s, axis=1, keepdims=True) * SCALE
    square_t = jnp.sum(wide_t * wide_t, axis=0, keepdims=True) * SCALE
    return jnp.exp2(dot(source_t, target) * (2.0 * SCALE) - (square_s + square_t))


def kernel(
    n_y, n_x, n_grp,
    points_hbm, charges_hbm, order_hbm, mask_ref, skel_hbm, interp_hbm, transfer_hbm,
    out_ref,
    pts, chg, order, skel, interp, transfer,
    pts_t, ordered, norm_t, near_pts, near_chg, near, back,
    coords, first, second, bundle, sib, cousin, top, far,
    load_sem, send_sem, recv_sem,
):
    leaf = lax.axis_index("leaf")
    grp = lax.axis_index("grp")
    core = leaf % 2
    other = 1 - core
    chip = leaf // 2
    y = chip % n_y
    x = chip // n_y
    odd = y % 2
    quarter = 2 * core + odd
    n_chip = n_x * n_y
    has_a = chip > 0
    has_b = chip < n_chip - 1

    def at_yx(yy, xx):
        return ((xx * n_y + (yy + n_y) % n_y) * 2 + core, grp)

    partner = (chip * 2 + other, grp)
    beside = at_yx(y + 1 - 2 * odd, x)
    across_x = (x + 2) % n_x
    family = {
        2: [
            at_yx(y + 2 - 4 * ((y // 2) % 2), x),
            at_yx(y - 2 + 4 * ((y // 2) % 2), x),
            at_yx(y + 4, x),
        ],
        4: [at_yx(y, x + 1 - 2 * (x % 2)), at_yx(y, n_x - 1 - x), at_yx(y, across_x)],
    }
    bits = [core, odd, (y // 2) % 2, (y // 4) % 2, x % 2, (x // 2) % 2]

    loads = [
        pltpu.make_async_copy(src, dst, load_sem.at[i])
        for i, (src, dst) in enumerate(
            [
                (order_hbm, order),
                (charges_hbm, chg),
                (interp_hbm, interp),
                (skel_hbm, skel),
                (points_hbm, pts),
                (transfer_hbm, transfer),
            ]
        )
    ]
    for load in loads:
        load.start()

    barrier = pltpu.get_barrier_semaphore()
    peers = [partner, beside] + family[2] + family[4] + [(leaf, (grp + step) % n_grp) for step in range(1, n_grp)]
    for peer in peers:
        pl.semaphore_signal(barrier, inc=1, device_id=peer, device_id_type=MESH)

    @pl.when(has_a)
    def _():
        pl.semaphore_signal(barrier, inc=1, device_id=(leaf - 2, grp), device_id_type=MESH)

    @pl.when(has_b)
    def _():
        pl.semaphore_signal(barrier, inc=1, device_id=(leaf + 2, grp), device_id_type=MESH)

    numbers = itertools.count()
    sent = []
    due = {}

    def remote(src, dst, send, recv, device):
        return pltpu.make_async_remote_copy(
            src_ref=src,
            dst_ref=dst,
            send_sem=send_sem.at[send],
            recv_sem=recv_sem.at[recv],
            device_id=device,
            device_id_type=MESH,
        )

    def when(condition, action):
        if condition is None:
            action()
        else:
            pl.when(condition)(action)

    def exchange(name, src, dst, arriving, device, send_if=None, due_if=None):
        number = next(numbers)
        copy = remote(src, dst, number, number, device)
        when(send_if, copy.start)
        sent.append((send_if, copy))
        due[name] = (due_if, remote(arriving, arriving, number, number, device))

    def arrive(name):
        condition, copy = due.pop(name)
        when(condition, copy.wait_recv)

    def finish():
        for name in list(due):
            arrive(name)
        for condition, copy in sent:
            when(condition, copy.wait_send)

    loads[0].wait()
    loads[1].wait()
    for column in range(0, LEAF, CHUNK):
        wanted = order[:, column : column + CHUNK]
        rows = lax.broadcasted_iota(jnp.int32, (LEAF, CHUNK), 0)
        pick = jnp.where(rows == wanted, 1.0, 0.0).astype(BF16)
        ordered[:, column : column + CHUNK] = dot(chg[...], pick).astype(BF16)
    loads[2].wait()
    weights = dot_nt(ordered[...], interp[...])
    loads[3].wait()
    loads[4].wait()
    rows = lax.broadcasted_iota(jnp.int32, (LEAF, SK), 0)
    pick = jnp.where(rows == skel[0], 1.0, 0.0).astype(BF16)
    coords[0] = dot(pts[...], pick).astype(BF16)
    loads[5].wait()

    def contribution(weights, level):
        high, low = split(weights)
        both = dot_nt(jnp.concatenate([high, low], axis=0), transfer[level])
        count = weights.shape[0]
        contrib = both[:count] + both[count:]
        return (*split(contrib), high, low), contrib

    def put(ref, index, values, rows):
        contrib_high, contrib_low, high, low = (v[rows] for v in values)
        ref[index, 0:PART_RHS] = contrib_high
        ref[index, PART_RHS:COORD] = contrib_low
        ref[index, WEIGHT:LOW] = high
        ref[index, LOW:BUNDLE] = low

    values, _ = contribution(weights, 0)
    for index in range(4):
        put(first, index, values, slice(index * PART_RHS, (index + 1) * PART_RHS))
        first[index, COORD:WEIGHT] = coords[0, index * PART_DIM : (index + 1) * PART_DIM]

    expected = len(peers) + has_a.astype(jnp.int32) + has_b.astype(jnp.int32)
    pl.semaphore_wait(barrier, expected)

    mine, theirs = pl.ds(2 * core, 2), pl.ds(2 * other, 2)
    exchange("first", first.at[theirs], sib.at[0, theirs], sib.at[0, mine], partner)
    exchange("first rest", first.at[mine], sib.at[0, mine], sib.at[0, theirs], partner)
    for row in range(0, LEAF, CHUNK):
        pts_t[row : row + CHUNK, :] = jnp.transpose(pts[:, row : row + CHUNK])
    exchange("p0", pts_t, near_pts.at[0], near_pts.at[0], partner)
    exchange("p1", ordered, near_chg.at[0], near_chg.at[0], partner)

    forth = 4 * core - 2
    onward, backward = (leaf + forth, grp), (leaf - forth, grp)
    to_there = jnp.where(core == 1, has_b, has_a)
    from_there = jnp.where(core == 1, has_a, has_b)
    piece_rows = LEAF // (N_PIECE - 2)
    pieces = iter(range(N_PIECE))

    def send_pieces(count):
        for index in itertools.islice(pieces, count):
            if index < 2:
                part = pl.ds(index * (RHS // 2), RHS // 2)
                source, target = ordered.at[part, :], near_chg.at[1, part, :]
            else:
                part = pl.ds((index - 2) * piece_rows, piece_rows)
                source, target = pts_t.at[part, :], near_pts.at[1, part, :]
            exchange(("near", index), source, target, target, onward, to_there, from_there)

    send_pieces(PIECES[0])
    wide = pts[...].astype(F32)
    norm_t[...] = jnp.sum(wide * wide, axis=0, keepdims=True) * SCALE
    near[...] = jnp.zeros_like(near)

    def near_tile(source_t, source_chg, keep, mirror=None):
        def body(step, carry):
            rows = pl.ds(pl.multiple_of(step * CHUNK, CHUNK), CHUNK)
            lhs = source_t[rows, :]
            wide = lhs.astype(F32)
            norm_s = jnp.sum(wide * wide, axis=1, keepdims=True) * SCALE
            charge = source_chg[:, rows]
            if keep is not None:
                charge = jnp.where(keep > 0, charge, jnp.zeros_like(charge))
            inner = dot(lhs, pts[...])
            tile = jnp.exp2(inner * (2.0 * SCALE) - (norm_s + norm_t[...])).astype(BF16)
            near[...] += dot(charge, tile)
            if mirror is not None:
                mirror[:, rows] = dot_nt(ordered[...], tile)
            return carry

        lax.fori_loop(0, LEAF // CHUNK, body, 0)

    def selection(level):
        wanted = skel[level + 1]
        rows = lax.broadcasted_iota(jnp.int32, (SK, SK), 0)
        upper = bits[level] * SK
        own = jnp.where(rows + upper == wanted, 1.0, 0.0).astype(BF16)
        far = jnp.where(rows + (SK - upper) == wanted, 1.0, 0.0).astype(BF16)
        return own, far

    def sib_coords(level):
        return jnp.concatenate([sib[level, q, COORD:WEIGHT, :] for q in range(4)], axis=0)

    def raise_part(level, own, there):
        pick_own, pick_far = selection(level)
        joined = dot(own[COORD:WEIGHT], pick_own) + dot(there[COORD:WEIGHT], pick_far)
        terms = [
            bundle_[rows].astype(F32)
            for bundle_ in (own, there)
            for rows in (slice(0, PART_RHS), slice(PART_RHS, COORD))
        ]
        return joined.astype(BF16), (terms[0] + terms[1]) + (terms[2] + terms[3])

    def raise_rest(level):
        own, far = selection(level)
        coords[level + 1] = (dot(coords[level], own) + dot(sib_coords(level), far)).astype(BF16)

    def sibling_field(level):
        source = jnp.transpose(sib_coords(level))
        kern_high, kern_low = split(pair_kernel(source, coords[level]))
        high = jnp.concatenate([sib[level, q, WEIGHT:LOW, :] for q in range(4)], axis=0)
        low = jnp.concatenate([sib[level, q, LOW:BUNDLE, :] for q in range(4)], axis=0)
        both = dot(jnp.concatenate([high, low], axis=0), kern_high)
        far[level] = both[:RHS] + both[RHS:] + dot(high, kern_low)

    lead = pl.ds(0, WEIGHT)
    tail = pl.ds(WEIGHT, BUNDLE - WEIGHT)
    body_rows = pl.ds(COORD, BUNDLE - COORD)

    def raise_first():
        results = [
            raise_part(0, first[2 * core + p], sib[0, 2 * core + p]) for p in range(2)
        ]
        values = contribution(jnp.concatenate([w for _, w in results], axis=0), 1)
        values = values[0]
        for p in range(2):
            put(second, p, values, slice(p * PART_RHS, (p + 1) * PART_RHS))
            second[p, COORD:WEIGHT] = results[p][0]

    def send_first():
        there, here = 2 * core + 1 - odd, 2 * core + odd
        exchange(
            ("main", 1), second.at[1 - odd, lead, :], sib.at[1, there, lead, :],
            sib.at[1, here, lead, :], beside,
        )
        exchange(
            ("tail", 1), second.at[1 - odd, tail, :], sib.at[1, there, tail, :],
            sib.at[1, here, tail, :], beside,
        )
        exchange(
            ("more", 1), second.at[odd, body_rows, :], sib.at[1, here, body_rows, :],
            sib.at[1, there, body_rows, :], beside,
        )

    def send_family(level, joined, weights):
        values, contrib = contribution(weights, level)
        put(bundle, level, values, slice(None))
        bundle[level, COORD:WEIGHT] = joined
        parent_values, _ = contribution(contrib, level + 1)
        put(bundle, level + 1, parent_values, slice(None))
        pick_own, _ = selection(level)
        bundle[level + 1, COORD:WEIGHT] = dot(joined, pick_own).astype(BF16)
        landing = sib.at[level, quarter]
        exchange(("sib", level), bundle.at[level], landing, landing, family[level][0])
        for index in range(2):
            landing = cousin.at[level // 4 * 2 + index]
            exchange(
                ("cousin", level, index), bundle.at[level + 1], landing, landing,
                family[level][1 + index],
            )

    def raise_family(level):
        arrive(("sib", level))
        joined, weights = raise_part(level, bundle[level], sib[level, quarter])
        _, contrib = contribution(weights, level + 1)
        own_pick, far_pick = selection(level + 1)
        arrive(("cousin", level, 0))
        arrive(("cousin", level, 1))
        parts = [cousin[level // 4 * 2 + index] for index in range(2)]
        coords_far = (
            parts[0][COORD:WEIGHT].astype(F32) + parts[1][COORD:WEIGHT].astype(F32)
        ).astype(BF16)
        above = (dot(joined, own_pick) + dot(coords_far, far_pick)).astype(BF16)
        contrib_far = sum_rows(parts, 0)
        return above, contrib + contrib_far, coords_far

    def sum_rows(parts, row):
        terms = [
            part[slice(row + shift, row + shift + PART_RHS)].astype(F32)
            for part in parts
            for shift in (0, PART_RHS)
        ]
        return (terms[0] + terms[1]) + (terms[2] + terms[3])

    def keep_cousins(level, coords_far):
        parts = [cousin[level // 4 * 2 + index] for index in range(2)]
        high, low = split(sum_rows(parts, WEIGHT))
        sib[level + 1, quarter, COORD:WEIGHT] = coords_far
        sib[level + 1, quarter, WEIGHT:LOW] = high
        sib[level + 1, quarter, LOW:BUNDLE] = low

    diagonal = 2 * core + 1 - odd
    across = 2 * other + odd
    corner = 2 * other + 1 - odd

    def spread(level):
        if level == 1:
            arrive(("tail", 1))
            arrive(("more", 1))
            exchange(
                ("core", level), sib.at[1, mine, body_rows, :], sib.at[1, mine, body_rows, :],
                sib.at[1, theirs, body_rows, :], partner,
            )
            return
        source = sib.at[level, quarter, body_rows, :]
        exchange(("core", level), source, source, sib.at[level, across, body_rows, :], partner)
        exchange(("side", level), source, source, sib.at[level, diagonal, body_rows, :], beside)

    def spread_side(level):
        arrive(("side", level))
        source = sib.at[level, diagonal, body_rows, :]
        exchange(("corner", level), source, source, sib.at[level, corner, body_rows, :], partner)

    def complete(level):
        arrive(("core", level))
        if level > 1:
            arrive(("corner", level))
        raise_rest(level)
        sibling_field(level)

    keep_p = jnp.where(core == 0, mask_ref[0, 3], mask_ref[0, 1])
    keep_f = jnp.where(core == 0, mask_ref[0, 1], mask_ref[0, 3])
    keep_in = jnp.where(core == 0, mask_ref[0, 4], mask_ref[0, 0])
    keep_out = jnp.where(core == 0, mask_ref[0, 0], mask_ref[0, 4])

    arrive("first")
    raise_first()
    send_first()
    send_pieces(PIECES[1])
    arrive("first rest")
    raise_rest(0)
    sibling_field(0)

    arrive(("main", 1))
    joined, weights = raise_part(1, second[odd], sib[1, quarter, 0:WEIGHT])
    send_family(2, joined, weights)
    send_pieces(PIECES[2])
    spread(1)
    near_tile(pts_t, ordered, None)
    complete(1)

    joined, weights, coords_far = raise_family(2)
    send_family(4, joined, weights)
    send_pieces(PIECES[3])
    keep_cousins(2, coords_far)
    spread(2)
    spread(3)
    for index in range(N_PIECE):
        arrive(("near", index))
    for name, ref in (("f0", near_pts), ("f1", near_chg)):
        exchange(name, ref.at[1], ref.at[2], ref.at[2], partner, from_there, to_there)

    @pl.when(from_there)
    def _():
        near_tile(near_pts.at[1], near_chg.at[1], keep_in, back.at[0])

    exchange("back", back.at[0], back.at[1], back.at[1], backward, from_there, to_there)

    joined, weights, coords_far = raise_family(4)
    bundle[LEVELS, COORD:WEIGHT] = joined
    bundle[LEVELS, WEIGHT:LOW] = weights.astype(BF16)

    steps = sorted(range(1, n_grp), key=lambda d: -min(d, n_grp - d))
    for step in steps:
        landing = top.at[step - 1, quarter]
        exchange(
            ("top", step), bundle.at[LEVELS, pl.ds(COORD, TOP), :], landing, landing,
            (leaf, (grp + step) % n_grp),
        )
    send_pieces(PIECES[4])
    keep_cousins(4, coords_far)
    spread(4)
    spread(5)
    spread_side(2)
    spread_side(3)
    arrive("p0")
    arrive("p1")
    near_tile(near_pts.at[0], near_chg.at[0], keep_p)
    complete(2)
    complete(3)

    def top_spread(step):
        arrive(("top", step))
        source = top.at[step - 1, quarter]
        exchange(("top core", step), source, source, top.at[step - 1, across], partner)
        exchange(("top side", step), source, source, top.at[step - 1, diagonal], beside)

    def top_spread_side(step):
        arrive(("top side", step))
        source = top.at[step - 1, diagonal]
        exchange(("top corner", step), source, source, top.at[step - 1, corner], partner)

    arrive("f0")
    arrive("f1")

    @pl.when(to_there)
    def _():
        near_tile(near_pts.at[2], near_chg.at[2], keep_f)

    for step in steps:
        top_spread(step)
    spread_side(4)
    spread_side(5)
    arrive("back")

    @pl.when(to_there)
    def _():
        near[...] += jnp.where(keep_out > 0, back[1], 0.0)

    for step in steps:
        top_spread_side(step)
    complete(4)
    complete(5)
    potential = jnp.zeros((RHS, SK), F32)
    for step in steps:
        arrive(("top core", step))
        arrive(("top corner", step))
        source = jnp.concatenate([top[step - 1, q, 0:PART_DIM, :] for q in range(4)], axis=0)
        kern_high, kern_low = split(pair_kernel(jnp.transpose(source), coords[LEVELS]))
        high = jnp.concatenate([top[step - 1, q, PART_DIM:TOP, :] for q in range(4)], axis=0)
        potential = potential + dot(high, kern_high) + dot(high, kern_low)

    def times(value, matrix):
        high, low = split(value)
        both = dot(jnp.concatenate([high, low], axis=0), matrix)
        return both[:RHS] + both[RHS:]

    for level in range(LEVELS - 1, -1, -1):
        potential = times(potential, transfer[level]) + far[level]
    out_ref[...] = near[...] + times(potential, interp[...])
    finish()


def solution(mesh):
    n_grp = mesh.shape["grp"]
    n_x, n_y = 4, mesh.shape["leaf"] // 8
    vmem = pltpu.VMEM

    def local(points, charges, order, near_mask, skeletons, leaf_interp, transfer):
        anywhere = pl.BlockSpec(memory_space=pltpu.HBM)
        return pl.pallas_call(
            functools.partial(kernel, n_y, n_x, n_grp),
            out_shape=jax.ShapeDtypeStruct((RHS, LEAF), F32),
            in_specs=[anywhere] * 3 + [pl.BlockSpec(memory_space=pltpu.SMEM)] + [anywhere] * 3,
            out_specs=pl.BlockSpec(memory_space=pltpu.VMEM),
            scratch_shapes=[
                vmem((DIM, LEAF), BF16),
                vmem((RHS, LEAF), BF16),
                vmem((1, LEAF), jnp.int32),
                vmem((LEVELS + 1, 1, SK), jnp.int32),
                vmem((SK, LEAF), BF16),
                vmem((LEVELS, SK, SK), BF16),
                vmem((LEAF, DIM), BF16),
                vmem((RHS, LEAF), BF16),
                vmem((1, LEAF), F32),
                vmem((3, LEAF, DIM), BF16),
                vmem((3, RHS, LEAF), BF16),
                vmem((RHS, LEAF), F32),
                vmem((2, RHS, LEAF), F32),
                vmem((LEVELS + 1, DIM, SK), BF16),
                vmem((4, BUNDLE, SK), BF16),
                vmem((2, BUNDLE, SK), BF16),
                vmem((LEVELS + 1, BUNDLE, SK), BF16),
                vmem((LEVELS, 4, BUNDLE, SK), BF16),
                vmem((4, BUNDLE, SK), BF16),
                vmem((n_grp - 1, 4, TOP, SK), BF16),
                vmem((LEVELS, RHS, SK), F32),
                pltpu.SemaphoreType.DMA((6,)),
                pltpu.SemaphoreType.DMA((96,)),
                pltpu.SemaphoreType.DMA((96,)),
            ],
            compiler_params=pltpu.CompilerParams(
                collective_id=0, has_side_effects=True, vmem_limit_bytes=67_043_328
            ),
        )(
            points,
            charges,
            order.reshape(1, LEAF),
            near_mask,
            jnp.transpose(skeletons, (1, 0, 2)),
            leaf_interp,
            transfer.reshape(LEVELS, SK, SK),
        )

    in_specs = (
        P(None, ("leaf", "grp")),
        P(None, ("leaf", "grp")),
        P(("leaf", "grp")),
        P(("leaf", "grp"), None),
        P(("leaf", "grp"), None, None),
        P(None, ("leaf", "grp")),
        P(("leaf", "grp"), None, None, None),
    )
    out_specs = P(None, ("leaf", "grp"))
    return jax.shard_map(local, mesh=mesh, in_specs=in_specs, out_specs=out_specs, check_vma=False)
```

```python
import functools
import itertools
import math

import jax
import jax.numpy as jnp
from jax import lax
from jax.experimental import pallas as pl
from jax.experimental.pallas import tpu as pltpu
from jax.sharding import PartitionSpec as P

MESH = pl.DeviceIdType.MESH
F32 = jnp.float32
BF16 = jnp.bfloat16
DIM, RHS, SK, LEAF, LEVELS = 256, 64, 128, 1024, 6
PART_DIM, PART_RHS = DIM // 4, RHS // 4
COORD = 2 * PART_RHS
WEIGHT = COORD + PART_DIM
LOW = WEIGHT + PART_RHS
BUNDLE = LOW + PART_RHS
TOP = PART_DIM + PART_RHS
SCALE = 2.0 / DIM / math.log(2.0)
CHUNK = 256
N_PIECE = 10
PIECES = (2, 2, 3, 3, 0)


def dot(a, b):
    return jnp.dot(a, b, preferred_element_type=F32)


def dot_nt(a, b):
    return lax.dot_general(a, b, (((1,), (1,)), ((), ())), preferred_element_type=F32)


def split(value):
    high = value.astype(BF16)
    low = (value - high.astype(F32)).astype(BF16)
    return high, low


def pair_kernel(source_t, target):
    wide_s = source_t.astype(F32)
    wide_t = target.astype(F32)
    square_s = jnp.sum(wide_s * wide_s, axis=1, keepdims=True) * SCALE
    square_t = jnp.sum(wide_t * wide_t, axis=0, keepdims=True) * SCALE
    return jnp.exp2(dot(source_t, target) * (2.0 * SCALE) - (square_s + square_t))


def kernel(
    n_y, n_x, n_grp,
    points_hbm, charges_hbm, order_hbm, mask_ref, skel_hbm, interp_hbm, transfer_hbm,
    out_ref,
    pts, chg, order, skel, interp, transfer,
    pts_t, ordered, norm_t, near_pts, near_chg, near, back,
    coords, first, second, bundle, sib, cousin, top, far,
    load_sem, send_sem, recv_sem,
):
    leaf = lax.axis_index("leaf")
    grp = lax.axis_index("grp")
    core = leaf % 2
    other = 1 - core
    chip = leaf // 2
    y = chip % n_y
    x = chip // n_y
    odd = y % 2
    quarter = 2 * core + odd
    n_chip = n_x * n_y
    has_a = chip > 0
    has_b = chip < n_chip - 1

    def at_yx(yy, xx):
        return ((xx * n_y + (yy + n_y) % n_y) * 2 + core, grp)

    partner = (chip * 2 + other, grp)
    beside = at_yx(y + 1 - 2 * odd, x)
    across_x = (x + 2) % n_x
    family = {
        2: [
            at_yx(y + 2 - 4 * ((y // 2) % 2), x),
            at_yx(y - 2 + 4 * ((y // 2) % 2), x),
            at_yx(y + 4, x),
        ],
        4: [at_yx(y, x + 1 - 2 * (x % 2)), at_yx(y, n_x - 1 - x), at_yx(y, across_x)],
    }
    bits = [core, odd, (y // 2) % 2, (y // 4) % 2, x % 2, (x // 2) % 2]

    loads = [
        pltpu.make_async_copy(src, dst, load_sem.at[i])
        for i, (src, dst) in enumerate(
            [
                (order_hbm, order),
                (charges_hbm, chg),
                (interp_hbm, interp),
                (skel_hbm, skel),
                (points_hbm, pts),
                (transfer_hbm, transfer),
            ]
        )
    ]
    for load in loads:
        load.start()

    barrier = pltpu.get_barrier_semaphore()
    peers = [partner, beside] + family[2] + family[4] + [(leaf, (grp + step) % n_grp) for step in range(1, n_grp)]
    for peer in peers:
        pl.semaphore_signal(barrier, inc=1, device_id=peer, device_id_type=MESH)

    @pl.when(has_a)
    def _():
        pl.semaphore_signal(barrier, inc=1, device_id=(leaf - 2, grp), device_id_type=MESH)

    @pl.when(has_b)
    def _():
        pl.semaphore_signal(barrier, inc=1, device_id=(leaf + 2, grp), device_id_type=MESH)

    numbers = itertools.count()
    sent = []
    due = {}

    def remote(src, dst, send, recv, device):
        return pltpu.make_async_remote_copy(
            src_ref=src,
            dst_ref=dst,
            send_sem=send_sem.at[send],
            recv_sem=recv_sem.at[recv],
            device_id=device,
            device_id_type=MESH,
        )

    def when(condition, action):
        if condition is None:
            action()
        else:
            pl.when(condition)(action)

    def exchange(name, src, dst, arriving, device, send_if=None, due_if=None):
        number = next(numbers)
        copy = remote(src, dst, number, number, device)
        when(send_if, copy.start)
        sent.append((send_if, copy))
        due[name] = (due_if, remote(arriving, arriving, number, number, device))

    def arrive(name):
        condition, copy = due.pop(name)
        when(condition, copy.wait_recv)

    def finish():
        for name in list(due):
            arrive(name)
        for condition, copy in sent:
            when(condition, copy.wait_send)

    loads[0].wait()
    loads[1].wait()
    for column in range(0, LEAF, CHUNK):
        wanted = order[:, column : column + CHUNK]
        rows = lax.broadcasted_iota(jnp.int32, (LEAF, CHUNK), 0)
        pick = jnp.where(rows == wanted, 1.0, 0.0).astype(BF16)
        ordered[:, column : column + CHUNK] = dot(chg[...], pick).astype(BF16)
    loads[2].wait()
    weights = dot_nt(ordered[...], interp[...])
    loads[3].wait()
    loads[4].wait()
    rows = lax.broadcasted_iota(jnp.int32, (LEAF, SK), 0)
    pick = jnp.where(rows == skel[0], 1.0, 0.0).astype(BF16)
    coords[0] = dot(pts[...], pick).astype(BF16)
    loads[5].wait()

    def contribution(weights, level):
        high, low = split(weights)
        both = dot_nt(jnp.concatenate([high, low], axis=0), transfer[level])
        count = weights.shape[0]
        contrib = both[:count] + both[count:]
        return (*split(contrib), high, low), contrib

    def put(ref, index, values, rows):
        contrib_high, contrib_low, high, low = (v[rows] for v in values)
        ref[index, 0:PART_RHS] = contrib_high
        ref[index, PART_RHS:COORD] = contrib_low
        ref[index, WEIGHT:LOW] = high
        ref[index, LOW:BUNDLE] = low

    values, _ = contribution(weights, 0)
    for index in range(4):
        put(first, index, values, slice(index * PART_RHS, (index + 1) * PART_RHS))
        first[index, COORD:WEIGHT] = coords[0, index * PART_DIM : (index + 1) * PART_DIM]

    expected = len(peers) + has_a.astype(jnp.int32) + has_b.astype(jnp.int32)
    pl.semaphore_wait(barrier, expected)

    mine, theirs = pl.ds(2 * core, 2), pl.ds(2 * other, 2)
    exchange("first", first.at[theirs], sib.at[0, theirs], sib.at[0, mine], partner)
    exchange("first rest", first.at[mine], sib.at[0, mine], sib.at[0, theirs], partner)

    forth = 4 * core - 2
    onward, backward = (leaf + forth, grp), (leaf - forth, grp)
    to_there = jnp.where(core == 1, has_b, has_a)
    from_there = jnp.where(core == 1, has_a, has_b)
    piece_rows = LEAF // (N_PIECE - 2)
    pieces = iter(range(N_PIECE))

    def send_pieces(count):
        for index in itertools.islice(pieces, count):
            if index < 2:
                part = pl.ds(index * (RHS // 2), RHS // 2)
                source, target = ordered.at[part, :], near_chg.at[1, part, :]
            else:
                part = pl.ds((index - 2) * piece_rows, piece_rows)
                source, target = pts_t.at[part, :], near_pts.at[1, part, :]
            exchange(("near", index), source, target, target, onward, to_there, from_there)


    def near_tile(source_t, source_chg, keep, mirror=None):
        def body(step, carry):
            rows = pl.ds(pl.multiple_of(step * CHUNK, CHUNK), CHUNK)
            lhs = source_t[rows, :]
            wide = lhs.astype(F32)
            norm_s = jnp.sum(wide * wide, axis=1, keepdims=True) * SCALE
            charge = source_chg[:, rows]
            if keep is not None:
                charge = jnp.where(keep > 0, charge, jnp.zeros_like(charge))
            inner = dot(lhs, pts[...])
            tile = jnp.exp2(inner * (2.0 * SCALE) - (norm_s + norm_t[...])).astype(BF16)
            near[...] += dot(charge, tile)
            if mirror is not None:
                mirror[:, rows] = dot_nt(ordered[...], tile)
            return carry

        lax.fori_loop(0, LEAF // CHUNK, body, 0)

    def selection(level):
        wanted = skel[level + 1]
        rows = lax.broadcasted_iota(jnp.int32, (SK, SK), 0)
        upper = bits[level] * SK
        own = jnp.where(rows + upper == wanted, 1.0, 0.0).astype(BF16)
        far = jnp.where(rows + (SK - upper) == wanted, 1.0, 0.0).astype(BF16)
        return own, far

    def sib_coords(level):
        return jnp.concatenate([sib[level, q, COORD:WEIGHT, :] for q in range(4)], axis=0)

    def raise_part(level, own, there):
        pick_own, pick_far = selection(level)
        joined = dot(own[COORD:WEIGHT], pick_own) + dot(there[COORD:WEIGHT], pick_far)
        terms = [
            bundle_[rows].astype(F32)
            for bundle_ in (own, there)
            for rows in (slice(0, PART_RHS), slice(PART_RHS, COORD))
        ]
        return joined.astype(BF16), (terms[0] + terms[1]) + (terms[2] + terms[3])

    def raise_rest(level):
        own, far = selection(level)
        coords[level + 1] = (dot(coords[level], own) + dot(sib_coords(level), far)).astype(BF16)

    def sibling_field(level):
        source = jnp.transpose(sib_coords(level))
        kern_high, kern_low = split(pair_kernel(source, coords[level]))
        high = jnp.concatenate([sib[level, q, WEIGHT:LOW, :] for q in range(4)], axis=0)
        low = jnp.concatenate([sib[level, q, LOW:BUNDLE, :] for q in range(4)], axis=0)
        both = dot(jnp.concatenate([high, low], axis=0), kern_high)
        far[level] = both[:RHS] + both[RHS:] + dot(high, kern_low)

    lead = pl.ds(0, WEIGHT)
    tail = pl.ds(WEIGHT, BUNDLE - WEIGHT)
    body_rows = pl.ds(COORD, BUNDLE - COORD)

    def raise_first():
        results = [
            raise_part(0, first[2 * core + p], sib[0, 2 * core + p]) for p in range(2)
        ]
        values = contribution(jnp.concatenate([w for _, w in results], axis=0), 1)
        values = values[0]
        for p in range(2):
            put(second, p, values, slice(p * PART_RHS, (p + 1) * PART_RHS))
            second[p, COORD:WEIGHT] = results[p][0]

    def send_first():
        there, here = 2 * core + 1 - odd, 2 * core + odd
        exchange(
            ("main", 1), second.at[1 - odd, lead, :], sib.at[1, there, lead, :],
            sib.at[1, here, lead, :], beside,
        )
        exchange(
            ("tail", 1), second.at[1 - odd, tail, :], sib.at[1, there, tail, :],
            sib.at[1, here, tail, :], beside,
        )
        exchange(
            ("more", 1), second.at[odd, body_rows, :], sib.at[1, here, body_rows, :],
            sib.at[1, there, body_rows, :], beside,
        )

    def send_family(level, joined, weights):
        values, contrib = contribution(weights, level)
        put(bundle, level, values, slice(None))
        bundle[level, COORD:WEIGHT] = joined
        parent_values, _ = contribution(contrib, level + 1)
        put(bundle, level + 1, parent_values, slice(None))
        pick_own, _ = selection(level)
        bundle[level + 1, COORD:WEIGHT] = dot(joined, pick_own).astype(BF16)
        landing = sib.at[level, quarter]
        exchange(("sib", level), bundle.at[level], landing, landing, family[level][0])
        for index in range(2):
            landing = cousin.at[level // 4 * 2 + index]
            exchange(
                ("cousin", level, index), bundle.at[level + 1], landing, landing,
                family[level][1 + index],
            )

    def raise_family(level):
        arrive(("sib", level))
        joined, weights = raise_part(level, bundle[level], sib[level, quarter])
        _, contrib = contribution(weights, level + 1)
        own_pick, far_pick = selection(level + 1)
        arrive(("cousin", level, 0))
        arrive(("cousin", level, 1))
        parts = [cousin[level // 4 * 2 + index] for index in range(2)]
        coords_far = (
            parts[0][COORD:WEIGHT].astype(F32) + parts[1][COORD:WEIGHT].astype(F32)
        ).astype(BF16)
        above = (dot(joined, own_pick) + dot(coords_far, far_pick)).astype(BF16)
        contrib_far = sum_rows(parts, 0)
        return above, contrib + contrib_far, coords_far

    def sum_rows(parts, row):
        terms = [
            part[slice(row + shift, row + shift + PART_RHS)].astype(F32)
            for part in parts
            for shift in (0, PART_RHS)
        ]
        return (terms[0] + terms[1]) + (terms[2] + terms[3])

    def keep_cousins(level, coords_far):
        parts = [cousin[level // 4 * 2 + index] for index in range(2)]
        high, low = split(sum_rows(parts, WEIGHT))
        sib[level + 1, quarter, COORD:WEIGHT] = coords_far
        sib[level + 1, quarter, WEIGHT:LOW] = high
        sib[level + 1, quarter, LOW:BUNDLE] = low

    diagonal = 2 * core + 1 - odd
    across = 2 * other + odd
    corner = 2 * other + 1 - odd

    def spread(level):
        if level == 1:
            arrive(("tail", 1))
            arrive(("more", 1))
            exchange(
                ("core", level), sib.at[1, mine, body_rows, :], sib.at[1, mine, body_rows, :],
                sib.at[1, theirs, body_rows, :], partner,
            )
            return
        source = sib.at[level, quarter, body_rows, :]
        exchange(("core", level), source, source, sib.at[level, across, body_rows, :], partner)
        exchange(("side", level), source, source, sib.at[level, diagonal, body_rows, :], beside)

    def spread_side(level):
        arrive(("side", level))
        source = sib.at[level, diagonal, body_rows, :]
        exchange(("corner", level), source, source, sib.at[level, corner, body_rows, :], partner)

    def complete(level):
        arrive(("core", level))
        if level > 1:
            arrive(("corner", level))
        raise_rest(level)
        sibling_field(level)

    keep_p = jnp.where(core == 0, mask_ref[0, 3], mask_ref[0, 1])
    keep_f = jnp.where(core == 0, mask_ref[0, 1], mask_ref[0, 3])
    keep_in = jnp.where(core == 0, mask_ref[0, 4], mask_ref[0, 0])
    keep_out = jnp.where(core == 0, mask_ref[0, 0], mask_ref[0, 4])

    arrive("first")
    raise_first()
    send_first()
    for row in range(0, LEAF, CHUNK):
        pts_t[row : row + CHUNK, :] = jnp.transpose(pts[:, row : row + CHUNK])
    exchange("p0", pts_t, near_pts.at[0], near_pts.at[0], partner)
    exchange("p1", ordered, near_chg.at[0], near_chg.at[0], partner)
    send_pieces(PIECES[0])
    wide = pts[...].astype(F32)
    norm_t[...] = jnp.sum(wide * wide, axis=0, keepdims=True) * SCALE
    near[...] = jnp.zeros_like(near)
    send_pieces(PIECES[1])
    arrive("first rest")
    raise_rest(0)
    sibling_field(0)

    arrive(("main", 1))
    joined, weights = raise_part(1, second[odd], sib[1, quarter, 0:WEIGHT])
    send_family(2, joined, weights)
    send_pieces(PIECES[2])
    spread(1)
    near_tile(pts_t, ordered, None)
    complete(1)

    joined, weights, coords_far = raise_family(2)
    send_family(4, joined, weights)
    send_pieces(PIECES[3])
    keep_cousins(2, coords_far)
    spread(2)
    spread(3)
    arrive("p0")
    arrive("p1")
    near_tile(near_pts.at[0], near_chg.at[0], keep_p)

    joined, weights, coords_far = raise_family(4)
    bundle[LEVELS, COORD:WEIGHT] = joined
    bundle[LEVELS, WEIGHT:LOW] = weights.astype(BF16)

    steps = sorted(range(1, n_grp), key=lambda d: -min(d, n_grp - d))
    for step in steps:
        landing = top.at[step - 1, quarter]
        exchange(
            ("top", step), bundle.at[LEVELS, pl.ds(COORD, TOP), :], landing, landing,
            (leaf, (grp + step) % n_grp),
        )
    send_pieces(PIECES[4])
    keep_cousins(4, coords_far)
    spread(4)
    spread(5)
    spread_side(2)
    spread_side(3)
    for index in range(N_PIECE):
        arrive(("near", index))
    for name, ref in (("f0", near_pts), ("f1", near_chg)):
        exchange(name, ref.at[1], ref.at[2], ref.at[2], partner, from_there, to_there)

    @pl.when(from_there)
    def _():
        near_tile(near_pts.at[1], near_chg.at[1], keep_in, back.at[0])

    exchange("back", back.at[0], back.at[1], back.at[1], backward, from_there, to_there)
    complete(2)
    complete(3)

    def top_spread(step):
        arrive(("top", step))
        source = top.at[step - 1, quarter]
        exchange(("top core", step), source, source, top.at[step - 1, across], partner)
        exchange(("top side", step), source, source, top.at[step - 1, diagonal], beside)

    def top_spread_side(step):
        arrive(("top side", step))
        source = top.at[step - 1, diagonal]
        exchange(("top corner", step), source, source, top.at[step - 1, corner], partner)

    arrive("f0")
    arrive("f1")

    @pl.when(to_there)
    def _():
        near_tile(near_pts.at[2], near_chg.at[2], keep_f)

    for step in steps:
        top_spread(step)
    spread_side(4)
    spread_side(5)
    arrive("back")

    @pl.when(to_there)
    def _():
        near[...] += jnp.where(keep_out > 0, back[1], 0.0)

    for step in steps:
        top_spread_side(step)
    complete(4)
    complete(5)
    potential = jnp.zeros((RHS, SK), F32)
    for step in steps:
        arrive(("top core", step))
        arrive(("top corner", step))
        source = jnp.concatenate([top[step - 1, q, 0:PART_DIM, :] for q in range(4)], axis=0)
        kern_high, kern_low = split(pair_kernel(jnp.transpose(source), coords[LEVELS]))
        high = jnp.concatenate([top[step - 1, q, PART_DIM:TOP, :] for q in range(4)], axis=0)
        potential = potential + dot(high, kern_high) + dot(high, kern_low)

    def times(value, matrix):
        high, low = split(value)
        both = dot(jnp.concatenate([high, low], axis=0), matrix)
        return both[:RHS] + both[RHS:]

    for level in range(LEVELS - 1, -1, -1):
        potential = times(potential, transfer[level]) + far[level]
    out_ref[...] = near[...] + times(potential, interp[...])
    finish()


def solution(mesh):
    n_grp = mesh.shape["grp"]
    n_x, n_y = 4, mesh.shape["leaf"] // 8
    vmem = pltpu.VMEM

    def local(points, charges, order, near_mask, skeletons, leaf_interp, transfer):
        anywhere = pl.BlockSpec(memory_space=pltpu.HBM)
        return pl.pallas_call(
            functools.partial(kernel, n_y, n_x, n_grp),
            out_shape=jax.ShapeDtypeStruct((RHS, LEAF), F32),
            in_specs=[anywhere] * 3 + [pl.BlockSpec(memory_space=pltpu.SMEM)] + [anywhere] * 3,
            out_specs=pl.BlockSpec(memory_space=pltpu.VMEM),
            scratch_shapes=[
                vmem((DIM, LEAF), BF16),
                vmem((RHS, LEAF), BF16),
                vmem((1, LEAF), jnp.int32),
                vmem((LEVELS + 1, 1, SK), jnp.int32),
                vmem((SK, LEAF), BF16),
                vmem((LEVELS, SK, SK), BF16),
                vmem((LEAF, DIM), BF16),
                vmem((RHS, LEAF), BF16),
                vmem((1, LEAF), F32),
                vmem((3, LEAF, DIM), BF16),
                vmem((3, RHS, LEAF), BF16),
                vmem((RHS, LEAF), F32),
                vmem((2, RHS, LEAF), F32),
                vmem((LEVELS + 1, DIM, SK), BF16),
                vmem((4, BUNDLE, SK), BF16),
                vmem((2, BUNDLE, SK), BF16),
                vmem((LEVELS + 1, BUNDLE, SK), BF16),
                vmem((LEVELS, 4, BUNDLE, SK), BF16),
                vmem((4, BUNDLE, SK), BF16),
                vmem((n_grp - 1, 4, TOP, SK), BF16),
                vmem((LEVELS, RHS, SK), F32),
                pltpu.SemaphoreType.DMA((6,)),
                pltpu.SemaphoreType.DMA((96,)),
                pltpu.SemaphoreType.DMA((96,)),
            ],
            compiler_params=pltpu.CompilerParams(
                collective_id=0, has_side_effects=True, vmem_limit_bytes=67_043_328
            ),
        )(
            points,
            charges,
            order.reshape(1, LEAF),
            near_mask,
            jnp.transpose(skeletons, (1, 0, 2)),
            leaf_interp,
            transfer.reshape(LEVELS, SK, SK),
        )

    in_specs = (
        P(None, ("leaf", "grp")),
        P(None, ("leaf", "grp")),
        P(("leaf", "grp")),
        P(("leaf", "grp"), None),
        P(("leaf", "grp"), None, None),
        P(None, ("leaf", "grp")),
        P(("leaf", "grp"), None, None, None),
    )
    out_specs = P(None, ("leaf", "grp"))
    return jax.shard_map(local, mesh=mesh, in_specs=in_specs, out_specs=out_specs, check_vma=False)
```

```python
import functools
import itertools
import math

import jax
import jax.numpy as jnp
from jax import lax
from jax.experimental import pallas as pl
from jax.experimental.pallas import tpu as pltpu
from jax.sharding import PartitionSpec as P

MESH = pl.DeviceIdType.MESH
F32 = jnp.float32
BF16 = jnp.bfloat16
DIM, RHS, SK, LEAF, LEVELS = 256, 64, 128, 1024, 6
PART_DIM, PART_RHS = DIM // 4, RHS // 4
COORD = 2 * PART_RHS
WEIGHT = COORD + PART_DIM
LOW = WEIGHT + PART_RHS
BUNDLE = LOW + PART_RHS
TOP = PART_DIM + PART_RHS
SCALE = 2.0 / DIM / math.log(2.0)
CHUNK = 256
N_PIECE = 10
PIECES = (2, 2, 3, 3, 0)


def dot(a, b):
    return jnp.dot(a, b, preferred_element_type=F32)


def dot_nt(a, b):
    return lax.dot_general(a, b, (((1,), (1,)), ((), ())), preferred_element_type=F32)


def split(value):
    high = value.astype(BF16)
    low = (value - high.astype(F32)).astype(BF16)
    return high, low


def pair_kernel(source_t, target):
    wide_s = source_t.astype(F32)
    wide_t = target.astype(F32)
    square_s = jnp.sum(wide_s * wide_s, axis=1, keepdims=True) * SCALE
    square_t = jnp.sum(wide_t * wide_t, axis=0, keepdims=True) * SCALE
    return jnp.exp2(dot(source_t, target) * (2.0 * SCALE) - (square_s + square_t))


def kernel(
    n_y, n_x, n_grp,
    points_hbm, charges_hbm, order_hbm, mask_ref, skel_hbm, interp_hbm, transfer_hbm,
    out_ref,
    pts, chg, order, skel, interp, transfer,
    pts_t, ordered, norm_t, near_pts, near_chg, near, back,
    coords, first, second, bundle, sib, cousin, top, far,
    load_sem, send_sem, recv_sem,
):
    leaf = lax.axis_index("leaf")
    grp = lax.axis_index("grp")
    core = leaf % 2
    other = 1 - core
    chip = leaf // 2
    y = chip % n_y
    x = chip // n_y
    odd = y % 2
    quarter = 2 * core + odd
    n_chip = n_x * n_y
    has_a = chip > 0
    has_b = chip < n_chip - 1

    def at_yx(yy, xx):
        return ((xx * n_y + (yy + n_y) % n_y) * 2 + core, grp)

    partner = (chip * 2 + other, grp)
    beside = at_yx(y + 1 - 2 * odd, x)
    across_x = (x + 2) % n_x
    family = {
        2: [
            at_yx(y + 2 - 4 * ((y // 2) % 2), x),
            at_yx(y - 2 + 4 * ((y // 2) % 2), x),
            at_yx(y + 4, x),
        ],
        4: [at_yx(y, x + 1 - 2 * (x % 2)), at_yx(y, n_x - 1 - x), at_yx(y, across_x)],
    }
    bits = [core, odd, (y // 2) % 2, (y // 4) % 2, x % 2, (x // 2) % 2]

    loads = [
        pltpu.make_async_copy(src, dst, load_sem.at[i])
        for i, (src, dst) in enumerate(
            [
                (order_hbm, order),
                (charges_hbm, chg),
                (interp_hbm, interp),
                (skel_hbm, skel),
                (points_hbm, pts),
                (transfer_hbm, transfer),
            ]
        )
    ]
    for load in loads:
        load.start()

    barrier = pltpu.get_barrier_semaphore()
    peers = [partner, beside] + family[2] + family[4] + [(leaf, (grp + step) % n_grp) for step in range(1, n_grp)]
    for peer in peers:
        pl.semaphore_signal(barrier, inc=1, device_id=peer, device_id_type=MESH)

    @pl.when(has_a)
    def _():
        pl.semaphore_signal(barrier, inc=1, device_id=(leaf - 2, grp), device_id_type=MESH)

    @pl.when(has_b)
    def _():
        pl.semaphore_signal(barrier, inc=1, device_id=(leaf + 2, grp), device_id_type=MESH)

    numbers = itertools.count()
    sent = []
    due = {}

    def remote(src, dst, send, recv, device):
        return pltpu.make_async_remote_copy(
            src_ref=src,
            dst_ref=dst,
            send_sem=send_sem.at[send],
            recv_sem=recv_sem.at[recv],
            device_id=device,
            device_id_type=MESH,
        )

    def when(condition, action):
        if condition is None:
            action()
        else:
            pl.when(condition)(action)

    def exchange(name, src, dst, arriving, device, send_if=None, due_if=None):
        number = next(numbers)
        copy = remote(src, dst, number, number, device)
        when(send_if, copy.start)
        sent.append((send_if, copy))
        due[name] = (due_if, remote(arriving, arriving, number, number, device))

    def arrive(name):
        condition, copy = due.pop(name)
        when(condition, copy.wait_recv)

    def finish():
        for name in list(due):
            arrive(name)
        for condition, copy in sent:
            when(condition, copy.wait_send)

    loads[0].wait()
    loads[1].wait()
    for column in range(0, LEAF, CHUNK):
        wanted = order[:, column : column + CHUNK]
        rows = lax.broadcasted_iota(jnp.int32, (LEAF, CHUNK), 0)
        pick = jnp.where(rows == wanted, 1.0, 0.0).astype(BF16)
        ordered[:, column : column + CHUNK] = dot(chg[...], pick).astype(BF16)
    loads[2].wait()
    weights = dot_nt(ordered[...], interp[...])
    loads[3].wait()
    loads[4].wait()
    rows = lax.broadcasted_iota(jnp.int32, (LEAF, SK), 0)
    pick = jnp.where(rows == skel[0], 1.0, 0.0).astype(BF16)
    coords[0] = dot(pts[...], pick).astype(BF16)
    loads[5].wait()

    def contribution(weights, level):
        high, low = split(weights)
        both = dot_nt(jnp.concatenate([high, low], axis=0), transfer[level])
        count = weights.shape[0]
        contrib = both[:count] + both[count:]
        return (*split(contrib), high, low), contrib

    def put(ref, index, values, rows):
        contrib_high, contrib_low, high, low = (v[rows] for v in values)
        ref[index, 0:PART_RHS] = contrib_high
        ref[index, PART_RHS:COORD] = contrib_low
        ref[index, WEIGHT:LOW] = high
        ref[index, LOW:BUNDLE] = low

    values, _ = contribution(weights, 0)
    for index in range(4):
        put(first, index, values, slice(index * PART_RHS, (index + 1) * PART_RHS))
        first[index, COORD:WEIGHT] = coords[0, index * PART_DIM : (index + 1) * PART_DIM]

    expected = len(peers) + has_a.astype(jnp.int32) + has_b.astype(jnp.int32)
    pl.semaphore_wait(barrier, expected)

    mine, theirs = pl.ds(2 * core, 2), pl.ds(2 * other, 2)
    exchange("first", first.at[theirs], sib.at[0, theirs], sib.at[0, mine], partner)
    exchange("first rest", first.at[mine], sib.at[0, mine], sib.at[0, theirs], partner)

    forth = 4 * core - 2
    onward, backward = (leaf + forth, grp), (leaf - forth, grp)
    to_there = jnp.where(core == 1, has_b, has_a)
    from_there = jnp.where(core == 1, has_a, has_b)
    piece_rows = LEAF // (N_PIECE - 2)
    pieces = iter(range(N_PIECE))

    def send_pieces(count):
        for index in itertools.islice(pieces, count):
            if index < 2:
                part = pl.ds(index * (RHS // 2), RHS // 2)
                source, target = ordered.at[part, :], near_chg.at[1, part, :]
            else:
                part = pl.ds((index - 2) * piece_rows, piece_rows)
                source, target = pts_t.at[part, :], near_pts.at[1, part, :]
            exchange(("near", index), source, target, target, onward, to_there, from_there)


    def near_tile(source_t, source_chg, keep, mirror=None):
        def body(step, carry):
            rows = pl.ds(pl.multiple_of(step * CHUNK, CHUNK), CHUNK)
            lhs = source_t[rows, :]
            wide = lhs.astype(F32)
            norm_s = jnp.sum(wide * wide, axis=1, keepdims=True) * SCALE
            charge = source_chg[:, rows]
            if keep is not None:
                charge = jnp.where(keep > 0, charge, jnp.zeros_like(charge))
            inner = dot(lhs, pts[...])
            tile = jnp.exp2(inner * (2.0 * SCALE) - (norm_s + norm_t[...])).astype(BF16)
            near[...] += dot(charge, tile)
            if mirror is not None:
                mirror[:, rows] = dot_nt(ordered[...], tile)
            return carry

        lax.fori_loop(0, LEAF // CHUNK, body, 0)

    def selection(level):
        wanted = skel[level + 1]
        rows = lax.broadcasted_iota(jnp.int32, (SK, SK), 0)
        upper = bits[level] * SK
        own = jnp.where(rows + upper == wanted, 1.0, 0.0).astype(BF16)
        far = jnp.where(rows + (SK - upper) == wanted, 1.0, 0.0).astype(BF16)
        return own, far

    def sib_coords(level):
        return jnp.concatenate([sib[level, q, COORD:WEIGHT, :] for q in range(4)], axis=0)

    def raise_part(level, own, there):
        pick_own, pick_far = selection(level)
        joined = dot(own[COORD:WEIGHT], pick_own) + dot(there[COORD:WEIGHT], pick_far)
        terms = [
            bundle_[rows].astype(F32)
            for bundle_ in (own, there)
            for rows in (slice(0, PART_RHS), slice(PART_RHS, COORD))
        ]
        return joined.astype(BF16), (terms[0] + terms[1]) + (terms[2] + terms[3])

    def raise_rest(level):
        own, far = selection(level)
        coords[level + 1] = (dot(coords[level], own) + dot(sib_coords(level), far)).astype(BF16)

    def sibling_field(level):
        source = jnp.transpose(sib_coords(level))
        kern_high, kern_low = split(pair_kernel(source, coords[level]))
        high = jnp.concatenate([sib[level, q, WEIGHT:LOW, :] for q in range(4)], axis=0)
        low = jnp.concatenate([sib[level, q, LOW:BUNDLE, :] for q in range(4)], axis=0)
        both = dot(jnp.concatenate([high, low], axis=0), kern_high)
        far[level] = both[:RHS] + both[RHS:] + dot(high, kern_low)

    lead = pl.ds(0, WEIGHT)
    tail = pl.ds(WEIGHT, BUNDLE - WEIGHT)
    body_rows = pl.ds(COORD, BUNDLE - COORD)

    def raise_first():
        results = [
            raise_part(0, first[2 * core + p], sib[0, 2 * core + p]) for p in range(2)
        ]
        values = contribution(jnp.concatenate([w for _, w in results], axis=0), 1)
        values = values[0]
        for p in range(2):
            put(second, p, values, slice(p * PART_RHS, (p + 1) * PART_RHS))
            second[p, COORD:WEIGHT] = results[p][0]

    def send_first():
        there, here = 2 * core + 1 - odd, 2 * core + odd
        exchange(
            ("main", 1), second.at[1 - odd, lead, :], sib.at[1, there, lead, :],
            sib.at[1, here, lead, :], beside,
        )
        exchange(
            ("tail", 1), second.at[1 - odd, tail, :], sib.at[1, there, tail, :],
            sib.at[1, here, tail, :], beside,
        )
        exchange(
            ("more", 1), second.at[odd, body_rows, :], sib.at[1, here, body_rows, :],
            sib.at[1, there, body_rows, :], beside,
        )

    def send_family(level, joined, weights):
        values, contrib = contribution(weights, level)
        put(bundle, level, values, slice(None))
        bundle[level, COORD:WEIGHT] = joined
        parent_values, _ = contribution(contrib, level + 1)
        put(bundle, level + 1, parent_values, slice(None))
        pick_own, _ = selection(level)
        bundle[level + 1, COORD:WEIGHT] = dot(joined, pick_own).astype(BF16)
        landing = sib.at[level, quarter]
        exchange(("sib", level), bundle.at[level], landing, landing, family[level][0])
        for index in range(2):
            landing = cousin.at[level // 4 * 2 + index]
            exchange(
                ("cousin", level, index), bundle.at[level + 1], landing, landing,
                family[level][1 + index],
            )

    def raise_family(level):
        arrive(("sib", level))
        joined, weights = raise_part(level, bundle[level], sib[level, quarter])
        _, contrib = contribution(weights, level + 1)
        own_pick, far_pick = selection(level + 1)
        arrive(("cousin", level, 0))
        arrive(("cousin", level, 1))
        parts = [cousin[level // 4 * 2 + index] for index in range(2)]
        coords_far = (
            parts[0][COORD:WEIGHT].astype(F32) + parts[1][COORD:WEIGHT].astype(F32)
        ).astype(BF16)
        above = (dot(joined, own_pick) + dot(coords_far, far_pick)).astype(BF16)
        contrib_far = sum_rows(parts, 0)
        return above, contrib + contrib_far, coords_far

    def sum_rows(parts, row):
        terms = [
            part[slice(row + shift, row + shift + PART_RHS)].astype(F32)
            for part in parts
            for shift in (0, PART_RHS)
        ]
        return (terms[0] + terms[1]) + (terms[2] + terms[3])

    def keep_cousins(level, coords_far):
        parts = [cousin[level // 4 * 2 + index] for index in range(2)]
        high, low = split(sum_rows(parts, WEIGHT))
        sib[level + 1, quarter, COORD:WEIGHT] = coords_far
        sib[level + 1, quarter, WEIGHT:LOW] = high
        sib[level + 1, quarter, LOW:BUNDLE] = low

    diagonal = 2 * core + 1 - odd
    across = 2 * other + odd
    corner = 2 * other + 1 - odd

    def spread(level):
        if level == 1:
            arrive(("tail", 1))
            arrive(("more", 1))
            exchange(
                ("core", level), sib.at[1, mine, body_rows, :], sib.at[1, mine, body_rows, :],
                sib.at[1, theirs, body_rows, :], partner,
            )
            return
        source = sib.at[level, quarter, body_rows, :]
        exchange(("core", level), source, source, sib.at[level, across, body_rows, :], partner)
        exchange(("side", level), source, source, sib.at[level, diagonal, body_rows, :], beside)

    def spread_side(level):
        arrive(("side", level))
        source = sib.at[level, diagonal, body_rows, :]
        exchange(("corner", level), source, source, sib.at[level, corner, body_rows, :], partner)

    def complete(level):
        arrive(("core", level))
        if level > 1:
            arrive(("corner", level))
        raise_rest(level)
        sibling_field(level)

    keep_p = jnp.where(core == 0, mask_ref[0, 3], mask_ref[0, 1])
    keep_f = jnp.where(core == 0, mask_ref[0, 1], mask_ref[0, 3])
    keep_in = jnp.where(core == 0, mask_ref[0, 4], mask_ref[0, 0])
    keep_out = jnp.where(core == 0, mask_ref[0, 0], mask_ref[0, 4])

    arrive("first")
    raise_first()
    send_first()
    for row in range(0, LEAF, CHUNK):
        pts_t[row : row + CHUNK, :] = jnp.transpose(pts[:, row : row + CHUNK])
    exchange("p0", pts_t, near_pts.at[0], near_pts.at[0], partner)
    exchange("p1", ordered, near_chg.at[0], near_chg.at[0], partner)
    send_pieces(PIECES[0])
    wide = pts[...].astype(F32)
    norm_t[...] = jnp.sum(wide * wide, axis=0, keepdims=True) * SCALE
    near[...] = jnp.zeros_like(near)
    send_pieces(PIECES[1])
    arrive("first rest")
    raise_rest(0)
    sibling_field(0)

    arrive(("main", 1))
    joined, weights = raise_part(1, second[odd], sib[1, quarter, 0:WEIGHT])
    send_family(2, joined, weights)
    send_pieces(PIECES[2])
    spread(1)
    near_tile(pts_t, ordered, None)
    complete(1)

    joined, weights, coords_far = raise_family(2)
    send_family(4, joined, weights)
    send_pieces(PIECES[3])
    keep_cousins(2, coords_far)
    spread(2)
    spread(3)
    arrive("p0")
    arrive("p1")
    near_tile(near_pts.at[0], near_chg.at[0], keep_p)

    joined, weights, coords_far = raise_family(4)
    bundle[LEVELS, COORD:WEIGHT] = joined
    bundle[LEVELS, WEIGHT:LOW] = weights.astype(BF16)

    steps = sorted(range(1, n_grp), key=lambda d: -min(d, n_grp - d))
    for step in steps:
        landing = top.at[step - 1, quarter]
        exchange(
            ("top", step), bundle.at[LEVELS, pl.ds(COORD, TOP), :], landing, landing,
            (leaf, (grp + step) % n_grp),
        )
    send_pieces(PIECES[4])
    keep_cousins(4, coords_far)
    spread(4)
    spread(5)
    spread_side(2)
    spread_side(3)
    for index in range(N_PIECE):
        arrive(("near", index))
    for name, ref in (("f0", near_pts), ("f1", near_chg)):
        exchange(name, ref.at[1], ref.at[2], ref.at[2], partner, from_there, to_there)

    @pl.when(from_there)
    def _():
        near_tile(near_pts.at[1], near_chg.at[1], keep_in, back.at[0])

    exchange("back", back.at[0], back.at[1], back.at[1], backward, from_there, to_there)
    complete(2)
    complete(3)

    def top_spread(step):
        arrive(("top", step))
        source = top.at[step - 1, quarter]
        exchange(("top core", step), source, source, top.at[step - 1, across], partner)
        exchange(("top side", step), source, source, top.at[step - 1, diagonal], beside)

    def top_spread_side(step):
        arrive(("top side", step))
        source = top.at[step - 1, diagonal]
        exchange(("top corner", step), source, source, top.at[step - 1, corner], partner)

    for step in steps:
        top_spread(step)
    spread_side(4)
    spread_side(5)
    arrive("f0")
    arrive("f1")

    @pl.when(to_there)
    def _():
        near_tile(near_pts.at[2], near_chg.at[2], keep_f)

    for step in steps:
        top_spread_side(step)
    complete(4)
    complete(5)
    potential = jnp.zeros((RHS, SK), F32)
    for step in steps:
        arrive(("top core", step))
        arrive(("top corner", step))
        source = jnp.concatenate([top[step - 1, q, 0:PART_DIM, :] for q in range(4)], axis=0)
        kern_high, kern_low = split(pair_kernel(jnp.transpose(source), coords[LEVELS]))
        high = jnp.concatenate([top[step - 1, q, PART_DIM:TOP, :] for q in range(4)], axis=0)
        potential = potential + dot(high, kern_high) + dot(high, kern_low)

    def times(value, matrix):
        high, low = split(value)
        both = dot(jnp.concatenate([high, low], axis=0), matrix)
        return both[:RHS] + both[RHS:]

    for level in range(LEVELS - 1, -1, -1):
        potential = times(potential, transfer[level]) + far[level]
    arrive("back")

    @pl.when(to_there)
    def _():
        near[...] += jnp.where(keep_out > 0, back[1], 0.0)

    out_ref[...] = near[...] + times(potential, interp[...])
    finish()


def solution(mesh):
    n_grp = mesh.shape["grp"]
    n_x, n_y = 4, mesh.shape["leaf"] // 8
    vmem = pltpu.VMEM

    def local(points, charges, order, near_mask, skeletons, leaf_interp, transfer):
        anywhere = pl.BlockSpec(memory_space=pltpu.HBM)
        return pl.pallas_call(
            functools.partial(kernel, n_y, n_x, n_grp),
            out_shape=jax.ShapeDtypeStruct((RHS, LEAF), F32),
            in_specs=[anywhere] * 3 + [pl.BlockSpec(memory_space=pltpu.SMEM)] + [anywhere] * 3,
            out_specs=pl.BlockSpec(memory_space=pltpu.VMEM),
            scratch_shapes=[
                vmem((DIM, LEAF), BF16),
                vmem((RHS, LEAF), BF16),
                vmem((1, LEAF), jnp.int32),
                vmem((LEVELS + 1, 1, SK), jnp.int32),
                vmem((SK, LEAF), BF16),
                vmem((LEVELS, SK, SK), BF16),
                vmem((LEAF, DIM), BF16),
                vmem((RHS, LEAF), BF16),
                vmem((1, LEAF), F32),
                vmem((3, LEAF, DIM), BF16),
                vmem((3, RHS, LEAF), BF16),
                vmem((RHS, LEAF), F32),
                vmem((2, RHS, LEAF), F32),
                vmem((LEVELS + 1, DIM, SK), BF16),
                vmem((4, BUNDLE, SK), BF16),
                vmem((2, BUNDLE, SK), BF16),
                vmem((LEVELS + 1, BUNDLE, SK), BF16),
                vmem((LEVELS, 4, BUNDLE, SK), BF16),
                vmem((4, BUNDLE, SK), BF16),
                vmem((n_grp - 1, 4, TOP, SK), BF16),
                vmem((LEVELS, RHS, SK), F32),
                pltpu.SemaphoreType.DMA((6,)),
                pltpu.SemaphoreType.DMA((96,)),
                pltpu.SemaphoreType.DMA((96,)),
            ],
            compiler_params=pltpu.CompilerParams(
                collective_id=0, has_side_effects=True, vmem_limit_bytes=67_043_328
            ),
        )(
            points,
            charges,
            order.reshape(1, LEAF),
            near_mask,
            jnp.transpose(skeletons, (1, 0, 2)),
            leaf_interp,
            transfer.reshape(LEVELS, SK, SK),
        )

    in_specs = (
        P(None, ("leaf", "grp")),
        P(None, ("leaf", "grp")),
        P(("leaf", "grp")),
        P(("leaf", "grp"), None),
        P(("leaf", "grp"), None, None),
        P(None, ("leaf", "grp")),
        P(("leaf", "grp"), None, None, None),
    )
    out_specs = P(None, ("leaf", "grp"))
    return jax.shard_map(local, mesh=mesh, in_specs=in_specs, out_specs=out_specs, check_vma=False)
```

```python
import functools
import itertools
import math

import jax
import jax.numpy as jnp
from jax import lax
from jax.experimental import pallas as pl
from jax.experimental.pallas import tpu as pltpu
from jax.sharding import PartitionSpec as P

MESH = pl.DeviceIdType.MESH
F32 = jnp.float32
BF16 = jnp.bfloat16
DIM, RHS, SK, LEAF, LEVELS = 256, 64, 128, 1024, 6
PART_DIM, PART_RHS = DIM // 4, RHS // 4
COORD = 2 * PART_RHS
WEIGHT = COORD + PART_DIM
LOW = WEIGHT + PART_RHS
BUNDLE = LOW + PART_RHS
TOP = PART_DIM + PART_RHS
SCALE = 2.0 / DIM / math.log(2.0)
CHUNK = 256
N_PIECE = 10
PIECES = (2, 2, 3, 3, 0)


def dot(a, b):
    return jnp.dot(a, b, preferred_element_type=F32)


def dot_nt(a, b):
    return lax.dot_general(a, b, (((1,), (1,)), ((), ())), preferred_element_type=F32)


def split(value):
    high = value.astype(BF16)
    low = (value - high.astype(F32)).astype(BF16)
    return high, low


def pair_kernel(source_t, target):
    wide_s = source_t.astype(F32)
    wide_t = target.astype(F32)
    square_s = jnp.sum(wide_s * wide_s, axis=1, keepdims=True) * SCALE
    square_t = jnp.sum(wide_t * wide_t, axis=0, keepdims=True) * SCALE
    return jnp.exp2(dot(source_t, target) * (2.0 * SCALE) - (square_s + square_t))


def kernel(
    n_y, n_x, n_grp,
    points_hbm, charges_hbm, order_hbm, mask_ref, skel_hbm, interp_hbm, transfer_hbm,
    out_ref,
    pts, chg, order, skel, interp, transfer,
    pts_t, ordered, norm_t, near_pts, near_chg, near, back,
    coords, first, second, bundle, sib, cousin, top, far,
    load_sem, send_sem, recv_sem,
):
    leaf = lax.axis_index("leaf")
    grp = lax.axis_index("grp")
    core = leaf % 2
    other = 1 - core
    chip = leaf // 2
    y = chip % n_y
    x = chip // n_y
    odd = y % 2
    quarter = 2 * core + odd
    n_chip = n_x * n_y
    has_a = chip > 0
    has_b = chip < n_chip - 1

    def at_yx(yy, xx):
        return ((xx * n_y + (yy + n_y) % n_y) * 2 + core, grp)

    partner = (chip * 2 + other, grp)
    beside = at_yx(y + 1 - 2 * odd, x)
    across_x = (x + 2) % n_x
    family = {
        2: [
            at_yx(y + 2 - 4 * ((y // 2) % 2), x),
            at_yx(y - 2 + 4 * ((y // 2) % 2), x),
            at_yx(y + 4, x),
        ],
        4: [at_yx(y, x + 1 - 2 * (x % 2)), at_yx(y, n_x - 1 - x), at_yx(y, across_x)],
    }
    bits = [core, odd, (y // 2) % 2, (y // 4) % 2, x % 2, (x // 2) % 2]

    loads = [
        pltpu.make_async_copy(src, dst, load_sem.at[i])
        for i, (src, dst) in enumerate(
            [
                (order_hbm, order),
                (charges_hbm, chg),
                (interp_hbm, interp),
                (skel_hbm, skel),
                (points_hbm, pts),
                (transfer_hbm, transfer),
            ]
        )
    ]
    for load in loads:
        load.start()

    barrier = pltpu.get_barrier_semaphore()
    peers = [partner, beside] + family[2] + family[4] + [(leaf, (grp + step) % n_grp) for step in range(1, n_grp)]
    for peer in peers:
        pl.semaphore_signal(barrier, inc=1, device_id=peer, device_id_type=MESH)

    @pl.when(has_a)
    def _():
        pl.semaphore_signal(barrier, inc=1, device_id=(leaf - 2, grp), device_id_type=MESH)

    @pl.when(has_b)
    def _():
        pl.semaphore_signal(barrier, inc=1, device_id=(leaf + 2, grp), device_id_type=MESH)

    numbers = itertools.count()
    sent = []
    due = {}

    def remote(src, dst, send, recv, device):
        return pltpu.make_async_remote_copy(
            src_ref=src,
            dst_ref=dst,
            send_sem=send_sem.at[send],
            recv_sem=recv_sem.at[recv],
            device_id=device,
            device_id_type=MESH,
        )

    def when(condition, action):
        if condition is None:
            action()
        else:
            pl.when(condition)(action)

    def exchange(name, src, dst, arriving, device, send_if=None, due_if=None):
        number = next(numbers)
        copy = remote(src, dst, number, number, device)
        when(send_if, copy.start)
        sent.append((send_if, copy))
        due[name] = (due_if, remote(arriving, arriving, number, number, device))

    def arrive(name):
        condition, copy = due.pop(name)
        when(condition, copy.wait_recv)

    def finish():
        for name in list(due):
            arrive(name)
        for condition, copy in sent:
            when(condition, copy.wait_send)

    loads[0].wait()
    loads[1].wait()
    for column in range(0, LEAF, CHUNK):
        wanted = order[:, column : column + CHUNK]
        rows = lax.broadcasted_iota(jnp.int32, (LEAF, CHUNK), 0)
        pick = jnp.where(rows == wanted, 1.0, 0.0).astype(BF16)
        ordered[:, column : column + CHUNK] = dot(chg[...], pick).astype(BF16)
    loads[2].wait()
    weights = dot_nt(ordered[...], interp[...])
    loads[3].wait()
    loads[4].wait()
    rows = lax.broadcasted_iota(jnp.int32, (LEAF, SK), 0)
    pick = jnp.where(rows == skel[0], 1.0, 0.0).astype(BF16)
    coords[0] = dot(pts[...], pick).astype(BF16)
    loads[5].wait()

    def contribution(weights, level):
        high, low = split(weights)
        both = dot_nt(jnp.concatenate([high, low], axis=0), transfer[level])
        count = weights.shape[0]
        contrib = both[:count] + both[count:]
        return (*split(contrib), high, low), contrib

    def put(ref, index, values, rows):
        contrib_high, contrib_low, high, low = (v[rows] for v in values)
        ref[index, 0:PART_RHS] = contrib_high
        ref[index, PART_RHS:COORD] = contrib_low
        ref[index, WEIGHT:LOW] = high
        ref[index, LOW:BUNDLE] = low

    values, _ = contribution(weights, 0)
    for index in range(4):
        put(first, index, values, slice(index * PART_RHS, (index + 1) * PART_RHS))
        first[index, COORD:WEIGHT] = coords[0, index * PART_DIM : (index + 1) * PART_DIM]

    expected = len(peers) + has_a.astype(jnp.int32) + has_b.astype(jnp.int32)
    pl.semaphore_wait(barrier, expected)

    mine, theirs = pl.ds(2 * core, 2), pl.ds(2 * other, 2)
    exchange("first", first.at[theirs], sib.at[0, theirs], sib.at[0, mine], partner)
    exchange("first rest", first.at[mine], sib.at[0, mine], sib.at[0, theirs], partner)

    forth = 4 * core - 2
    onward, backward = (leaf + forth, grp), (leaf - forth, grp)
    to_there = jnp.where(core == 1, has_b, has_a)
    from_there = jnp.where(core == 1, has_a, has_b)
    piece_rows = LEAF // (N_PIECE - 2)
    pieces = iter(range(N_PIECE))

    def send_pieces(count):
        for index in itertools.islice(pieces, count):
            if index < 2:
                part = pl.ds(index * (RHS // 2), RHS // 2)
                source, target = ordered.at[part, :], near_chg.at[1, part, :]
            else:
                part = pl.ds((index - 2) * piece_rows, piece_rows)
                source, target = pts_t.at[part, :], near_pts.at[1, part, :]
            exchange(("near", index), source, target, target, onward, to_there, from_there)


    def near_tile(source_t, source_chg, keep, mirror=None):
        def body(step, carry):
            rows = pl.ds(pl.multiple_of(step * CHUNK, CHUNK), CHUNK)
            lhs = source_t[rows, :]
            wide = lhs.astype(F32)
            norm_s = jnp.sum(wide * wide, axis=1, keepdims=True) * SCALE
            charge = source_chg[:, rows]
            if keep is not None:
                charge = jnp.where(keep > 0, charge, jnp.zeros_like(charge))
            inner = dot(lhs, pts[...])
            tile = jnp.exp2(inner * (2.0 * SCALE) - (norm_s + norm_t[...])).astype(BF16)
            near[...] += dot(charge, tile)
            if mirror is not None:
                mirror[:, rows] = dot_nt(ordered[...], tile)
            return carry

        lax.fori_loop(0, LEAF // CHUNK, body, 0)

    def selection(level):
        wanted = skel[level + 1]
        rows = lax.broadcasted_iota(jnp.int32, (SK, SK), 0)
        upper = bits[level] * SK
        own = jnp.where(rows + upper == wanted, 1.0, 0.0).astype(BF16)
        far = jnp.where(rows + (SK - upper) == wanted, 1.0, 0.0).astype(BF16)
        return own, far

    def sib_coords(level):
        return jnp.concatenate([sib[level, q, COORD:WEIGHT, :] for q in range(4)], axis=0)

    def raise_part(level, own, there):
        pick_own, pick_far = selection(level)
        joined = dot(own[COORD:WEIGHT], pick_own) + dot(there[COORD:WEIGHT], pick_far)
        terms = [
            bundle_[rows].astype(F32)
            for bundle_ in (own, there)
            for rows in (slice(0, PART_RHS), slice(PART_RHS, COORD))
        ]
        return joined.astype(BF16), (terms[0] + terms[1]) + (terms[2] + terms[3])

    def raise_rest(level):
        own, far = selection(level)
        coords[level + 1] = (dot(coords[level], own) + dot(sib_coords(level), far)).astype(BF16)

    def sibling_field(level):
        source = jnp.transpose(sib_coords(level))
        kern_high, kern_low = split(pair_kernel(source, coords[level]))
        high = jnp.concatenate([sib[level, q, WEIGHT:LOW, :] for q in range(4)], axis=0)
        low = jnp.concatenate([sib[level, q, LOW:BUNDLE, :] for q in range(4)], axis=0)
        both = dot(jnp.concatenate([high, low], axis=0), kern_high)
        far[level] = both[:RHS] + both[RHS:] + dot(high, kern_low)

    lead = pl.ds(0, WEIGHT)
    tail = pl.ds(WEIGHT, BUNDLE - WEIGHT)
    body_rows = pl.ds(COORD, BUNDLE - COORD)

    def raise_first():
        results = [
            raise_part(0, first[2 * core + p], sib[0, 2 * core + p]) for p in range(2)
        ]
        values = contribution(jnp.concatenate([w for _, w in results], axis=0), 1)
        values = values[0]
        for p in range(2):
            put(second, p, values, slice(p * PART_RHS, (p + 1) * PART_RHS))
            second[p, COORD:WEIGHT] = results[p][0]

    def send_first():
        there, here = 2 * core + 1 - odd, 2 * core + odd
        exchange(
            ("main", 1), second.at[1 - odd, lead, :], sib.at[1, there, lead, :],
            sib.at[1, here, lead, :], beside,
        )
        exchange(
            ("tail", 1), second.at[1 - odd, tail, :], sib.at[1, there, tail, :],
            sib.at[1, here, tail, :], beside,
        )
        exchange(
            ("more", 1), second.at[odd, body_rows, :], sib.at[1, here, body_rows, :],
            sib.at[1, there, body_rows, :], beside,
        )

    def send_family(level, joined, weights):
        values, contrib = contribution(weights, level)
        put(bundle, level, values, slice(None))
        bundle[level, COORD:WEIGHT] = joined
        parent_values, _ = contribution(contrib, level + 1)
        put(bundle, level + 1, parent_values, slice(None))
        pick_own, _ = selection(level)
        bundle[level + 1, COORD:WEIGHT] = dot(joined, pick_own).astype(BF16)
        landing = sib.at[level, quarter]
        exchange(("sib", level), bundle.at[level], landing, landing, family[level][0])
        for index in range(2):
            landing = cousin.at[level // 4 * 2 + index]
            exchange(
                ("cousin", level, index), bundle.at[level + 1], landing, landing,
                family[level][1 + index],
            )

    def raise_family(level):
        arrive(("sib", level))
        joined, weights = raise_part(level, bundle[level], sib[level, quarter])
        _, contrib = contribution(weights, level + 1)
        own_pick, far_pick = selection(level + 1)
        arrive(("cousin", level, 0))
        arrive(("cousin", level, 1))
        parts = [cousin[level // 4 * 2 + index] for index in range(2)]
        coords_far = (
            parts[0][COORD:WEIGHT].astype(F32) + parts[1][COORD:WEIGHT].astype(F32)
        ).astype(BF16)
        above = (dot(joined, own_pick) + dot(coords_far, far_pick)).astype(BF16)
        contrib_far = sum_rows(parts, 0)
        return above, contrib + contrib_far, coords_far

    def sum_rows(parts, row):
        terms = [
            part[slice(row + shift, row + shift + PART_RHS)].astype(F32)
            for part in parts
            for shift in (0, PART_RHS)
        ]
        return (terms[0] + terms[1]) + (terms[2] + terms[3])

    def keep_cousins(level, coords_far):
        parts = [cousin[level // 4 * 2 + index] for index in range(2)]
        high, low = split(sum_rows(parts, WEIGHT))
        sib[level + 1, quarter, COORD:WEIGHT] = coords_far
        sib[level + 1, quarter, WEIGHT:LOW] = high
        sib[level + 1, quarter, LOW:BUNDLE] = low

    diagonal = 2 * core + 1 - odd
    across = 2 * other + odd
    corner = 2 * other + 1 - odd

    def spread(level):
        if level == 1:
            arrive(("tail", 1))
            arrive(("more", 1))
            exchange(
                ("core", level), sib.at[1, mine, body_rows, :], sib.at[1, mine, body_rows, :],
                sib.at[1, theirs, body_rows, :], partner,
            )
            return
        source = sib.at[level, quarter, body_rows, :]
        exchange(("core", level), source, source, sib.at[level, across, body_rows, :], partner)
        exchange(("side", level), source, source, sib.at[level, diagonal, body_rows, :], beside)

    def spread_side(level):
        arrive(("side", level))
        source = sib.at[level, diagonal, body_rows, :]
        exchange(("corner", level), source, source, sib.at[level, corner, body_rows, :], partner)

    def complete(level):
        arrive(("core", level))
        if level > 1:
            arrive(("corner", level))
        raise_rest(level)
        sibling_field(level)

    keep_p = jnp.where(core == 0, mask_ref[0, 3], mask_ref[0, 1])
    keep_f = jnp.where(core == 0, mask_ref[0, 1], mask_ref[0, 3])
    keep_in = jnp.where(core == 0, mask_ref[0, 4], mask_ref[0, 0])
    keep_out = jnp.where(core == 0, mask_ref[0, 0], mask_ref[0, 4])

    arrive("first")
    raise_first()
    send_first()
    for row in range(0, LEAF, CHUNK):
        pts_t[row : row + CHUNK, :] = jnp.transpose(pts[:, row : row + CHUNK])
    exchange("p0", pts_t, near_pts.at[0], near_pts.at[0], partner)
    exchange("p1", ordered, near_chg.at[0], near_chg.at[0], partner)
    send_pieces(PIECES[0])
    wide = pts[...].astype(F32)
    norm_t[...] = jnp.sum(wide * wide, axis=0, keepdims=True) * SCALE
    near[...] = jnp.zeros_like(near)
    send_pieces(PIECES[1])
    arrive("first rest")
    raise_rest(0)
    sibling_field(0)

    arrive(("main", 1))
    joined, weights = raise_part(1, second[odd], sib[1, quarter, 0:WEIGHT])
    send_family(2, joined, weights)
    send_pieces(PIECES[2])
    spread(1)
    near_tile(pts_t, ordered, None)
    complete(1)

    joined, weights, coords_far = raise_family(2)
    send_family(4, joined, weights)
    send_pieces(PIECES[3])
    keep_cousins(2, coords_far)
    spread(2)
    spread(3)
    arrive("p0")
    arrive("p1")
    near_tile(near_pts.at[0], near_chg.at[0], keep_p)

    joined, weights, coords_far = raise_family(4)
    bundle[LEVELS, COORD:WEIGHT] = joined
    bundle[LEVELS, WEIGHT:LOW] = weights.astype(BF16)

    steps = sorted(range(1, n_grp), key=lambda d: -min(d, n_grp - d))
    for step in steps:
        landing = top.at[step - 1, quarter]
        exchange(
            ("top", step), bundle.at[LEVELS, pl.ds(COORD, TOP), :], landing, landing,
            (leaf, (grp + step) % n_grp),
        )
    send_pieces(PIECES[4])
    keep_cousins(4, coords_far)
    spread(4)
    spread(5)
    spread_side(2)
    spread_side(3)
    for index in range(N_PIECE):
        arrive(("near", index))
    for name, ref in (("f0", near_pts), ("f1", near_chg)):
        exchange(name, ref.at[1], ref.at[2], ref.at[2], partner, from_there, to_there)

    @pl.when(from_there)
    def _():
        near_tile(near_pts.at[1], near_chg.at[1], keep_in, back.at[0])

    exchange("back", back.at[0], back.at[1], back.at[1], backward, from_there, to_there)

    def top_spread(step):
        arrive(("top", step))
        source = top.at[step - 1, quarter]
        exchange(("top core", step), source, source, top.at[step - 1, across], partner)
        exchange(("top side", step), source, source, top.at[step - 1, diagonal], beside)

    def top_spread_side(step):
        arrive(("top side", step))
        source = top.at[step - 1, diagonal]
        exchange(("top corner", step), source, source, top.at[step - 1, corner], partner)

    for step in steps:
        top_spread(step)
    spread_side(4)
    spread_side(5)
    complete(2)
    complete(3)
    arrive("f0")
    arrive("f1")

    @pl.when(to_there)
    def _():
        near_tile(near_pts.at[2], near_chg.at[2], keep_f)

    for step in steps:
        top_spread_side(step)
    complete(4)
    complete(5)
    potential = jnp.zeros((RHS, SK), F32)
    for step in steps:
        arrive(("top core", step))
        arrive(("top corner", step))
        source = jnp.concatenate([top[step - 1, q, 0:PART_DIM, :] for q in range(4)], axis=0)
        kern_high, kern_low = split(pair_kernel(jnp.transpose(source), coords[LEVELS]))
        high = jnp.concatenate([top[step - 1, q, PART_DIM:TOP, :] for q in range(4)], axis=0)
        potential = potential + dot(high, kern_high) + dot(high, kern_low)

    def times(value, matrix):
        high, low = split(value)
        both = dot(jnp.concatenate([high, low], axis=0), matrix)
        return both[:RHS] + both[RHS:]

    for level in range(LEVELS - 1, -1, -1):
        potential = times(potential, transfer[level]) + far[level]
    arrive("back")

    @pl.when(to_there)
    def _():
        near[...] += jnp.where(keep_out > 0, back[1], 0.0)

    out_ref[...] = near[...] + times(potential, interp[...])
    finish()


def solution(mesh):
    n_grp = mesh.shape["grp"]
    n_x, n_y = 4, mesh.shape["leaf"] // 8
    vmem = pltpu.VMEM

    def local(points, charges, order, near_mask, skeletons, leaf_interp, transfer):
        anywhere = pl.BlockSpec(memory_space=pltpu.HBM)
        return pl.pallas_call(
            functools.partial(kernel, n_y, n_x, n_grp),
            out_shape=jax.ShapeDtypeStruct((RHS, LEAF), F32),
            in_specs=[anywhere] * 3 + [pl.BlockSpec(memory_space=pltpu.SMEM)] + [anywhere] * 3,
            out_specs=pl.BlockSpec(memory_space=pltpu.VMEM),
            scratch_shapes=[
                vmem((DIM, LEAF), BF16),
                vmem((RHS, LEAF), BF16),
                vmem((1, LEAF), jnp.int32),
                vmem((LEVELS + 1, 1, SK), jnp.int32),
                vmem((SK, LEAF), BF16),
                vmem((LEVELS, SK, SK), BF16),
                vmem((LEAF, DIM), BF16),
                vmem((RHS, LEAF), BF16),
                vmem((1, LEAF), F32),
                vmem((3, LEAF, DIM), BF16),
                vmem((3, RHS, LEAF), BF16),
                vmem((RHS, LEAF), F32),
                vmem((2, RHS, LEAF), F32),
                vmem((LEVELS + 1, DIM, SK), BF16),
                vmem((4, BUNDLE, SK), BF16),
                vmem((2, BUNDLE, SK), BF16),
                vmem((LEVELS + 1, BUNDLE, SK), BF16),
                vmem((LEVELS, 4, BUNDLE, SK), BF16),
                vmem((4, BUNDLE, SK), BF16),
                vmem((n_grp - 1, 4, TOP, SK), BF16),
                vmem((LEVELS, RHS, SK), F32),
                pltpu.SemaphoreType.DMA((6,)),
                pltpu.SemaphoreType.DMA((96,)),
                pltpu.SemaphoreType.DMA((96,)),
            ],
            compiler_params=pltpu.CompilerParams(
                collective_id=0, has_side_effects=True, vmem_limit_bytes=67_043_328
            ),
        )(
            points,
            charges,
            order.reshape(1, LEAF),
            near_mask,
            jnp.transpose(skeletons, (1, 0, 2)),
            leaf_interp,
            transfer.reshape(LEVELS, SK, SK),
        )

    in_specs = (
        P(None, ("leaf", "grp")),
        P(None, ("leaf", "grp")),
        P(("leaf", "grp")),
        P(("leaf", "grp"), None),
        P(("leaf", "grp"), None, None),
        P(None, ("leaf", "grp")),
        P(("leaf", "grp"), None, None, None),
    )
    out_specs = P(None, ("leaf", "grp"))
    return jax.shard_map(local, mesh=mesh, in_specs=in_specs, out_specs=out_specs, check_vma=False)
```
